256 devices in a mesh: row: 8 (over x, core), rhs: 32 (over y, z).
Axes of the slice: x: 4, y: 4, z: 8, core: 2. Of those that a mesh axis runs over, the one named last changes fastest.
Arguments:
- local_rhs: bfloat16 [336, 128, 4096], P('row', None, 'rhs'), may hold values from -6 to 6
- top_rhs: bfloat16 [8, 128, 4096], P('row', None, 'rhs'), may hold values from -6 to 6
- diag_inv: bfloat16 [336, 128, 128], P('row', 'rhs'), as said below
- top_inv: bfloat16 [8, 128, 128], P('row', 'rhs'), as said below
- off_blocks: bfloat16 [336, 4, 128, 128], P('row', None, 'rhs'), may hold values from -0.125 to 0.125
- top_factor: bfloat16 [8, 8, 128, 128], P('row', None, 'rhs'), may hold values from -0.1875 to 0.1875
- targets: int32 [336, 4], P('row'), may hold values from 24 to 49, as said below
Outputs:
- local_solution: bfloat16 [336, 128, 4096], P('row', None, 'rhs')
- top_solution: bfloat16 [8, 128, 4096], P('row', None, 'rhs')
The draws below stay inside these ranges and needn't reach their ends.
Inputs may be any that keep to these rules, and one draw needn't show every extreme that they name: `diag_inv`: each block is lower triangular. `top_inv`: each block is lower triangular. `targets`: row r * 42 + k holds 4 distinct codes; a code c < 42 names local supernode r * 42 + c, of a higher level than k; a code c >= 42 names top block c - 42.
All inputs are finite; a program needn't handle non-finite values.
Results may differ from the reference program's by a relative error of at most 0.023.
Values may be sent and summed in bfloat16 or wider, within the bound.
No kernel may reach another device: no remote copies, remote signals or barrier semaphores. Data moves between devices by JAX's collectives and lax.ppermute only.
A program may use at most 64 MiB of HBM per device.

```python
import math
import jax
import jax.numpy as jnp
from jax import lax

B = 128
NB = 4
LEAF = 24
RHS_DEV = 128
SUB = 42
NLOC = 336
TOP = 8
NRHS = 4096
N_ROW = 8
N_RHS = 32


def lower_inverse(key, count):
    scales = jax.random.uniform(jax.random.fold_in(key, 11), (count, B), jnp.float32, 0.7, 1.3)
    noise = jax.random.normal(jax.random.fold_in(key, 12), (count, B, B), jnp.float32) * (0.6 / math.sqrt(B))
    lower = jnp.tril(noise, -1) + scales[:, :, None] * jnp.eye(B, dtype=jnp.float32)[None]
    return lower.astype(jnp.bfloat16)


def draw_diag_inv(key, part):
    return lower_inverse(key, SUB * N_ROW)


def draw_top_inv(key, part):
    return lower_inverse(key, N_ROW)


def draw_targets(key, part):
    cand_count = SUB + TOP
    local_index = jnp.arange(SUB, dtype=jnp.int32)
    next_level = jnp.where(local_index < LEAF, LEAF, jnp.where(local_index < LEAF + LEAF // 2, LEAF + LEAF // 2, SUB))
    candidate = jnp.arange(cand_count, dtype=jnp.int32)
    allowed = candidate[None, :] >= next_level[:, None]
    scores = jax.random.randint(jax.random.fold_in(key, 21), (N_ROW, SUB, cand_count), 0, 1 << 20, dtype=jnp.int32) * cand_count + candidate
    scores = jnp.where(allowed[None], scores, -1)
    chosen = lax.top_k(scores, NB)[1]
    return chosen.reshape(N_ROW * SUB, NB).astype(jnp.int32)


def level_of(key, shape, shards, least, high):
    factor_of, own = 1.0, jax.random.fold_in(key, 6)
    for dim, shards_of in shards:
        draws = jnp.exp(jax.random.uniform(jax.random.fold_in(own, dim), (shards_of,), jnp.float32, least / len(shards), high / len(shards)))
        factor_of = factor_of * jnp.repeat(draws, shape[dim] // shards_of).reshape([-1 if axis == dim else 1 for axis in range(len(shape))])
    return factor_of


def bell_draw(stream_key, extent, scale, bound, shards=(), kind=jnp.bfloat16):
    drawn = scale * jax.random.normal(stream_key, extent, jnp.float32)
    if shards:
        drawn = drawn * level_of(stream_key, extent, shards, -0.22, 0.18)
    return jnp.clip(drawn, -bound, bound).astype(kind)


def setup_inputs(seed: int = 0) -> dict:
    arg_keys = jax.random.split(jax.random.key(seed), 8)
    return {
        "local_rhs": bell_draw(arg_keys[0], (NLOC, B, NRHS), 1.0, 6.0, ((0, 8), (2, 32))),
        "top_rhs": bell_draw(arg_keys[1], (TOP, B, NRHS), 1.0, 6.0, ((0, 8), (2, 32))),
        "diag_inv": draw_diag_inv(jax.random.fold_in(arg_keys[7], 71), 0),
        "top_inv": draw_top_inv(jax.random.fold_in(arg_keys[7], 71), 0),
        "off_blocks": bell_draw(arg_keys[4], (NLOC, NB, B, B), (B * 16) ** -0.5, 0.125, ((0, 8), (2, 32))),
        "top_factor": bell_draw(arg_keys[5], (TOP, TOP, B, B), (B * TOP) ** -0.5, 0.1875, ((0, 8), (2, 32))),
        "targets": draw_targets(jax.random.fold_in(arg_keys[7], 71), 0),
    }


def reference(local_rhs, top_rhs, diag_inv, top_inv, off_blocks, top_factor, targets):
    inverse = diag_inv.reshape(N_ROW, SUB, B, B).astype(jnp.float32)
    blocks = off_blocks.reshape(N_ROW, SUB, NB, B, B).astype(jnp.float32)
    codes = targets.reshape(N_ROW, SUB, NB).astype(jnp.int32)
    owner = jnp.broadcast_to(jnp.arange(N_ROW, dtype=jnp.int32)[:, None, None], codes.shape)
    level_ranges = ((0, LEAF), (LEAF, LEAF + LEAF // 2), (LEAF + LEAF // 2, SUB))

    def solve_panel(panel_args):
        local_panel, top_panel = panel_args
        rows_all = local_panel.reshape(N_ROW, SUB, B, RHS_DEV)
        acc_local = jnp.zeros((N_ROW, SUB, B, RHS_DEV), jnp.float32)
        acc_top = jnp.zeros((TOP, B, RHS_DEV), jnp.float32)
        solved = []
        for first_row, end_row in level_ranges:
            residual_rows = (rows_all[:, first_row:end_row].astype(jnp.float32) - acc_local[:, first_row:end_row]).astype(jnp.bfloat16)
            level_partial = jnp.einsum("rsab,rsbp->rsap", inverse[:, first_row:end_row], residual_rows.astype(jnp.float32)).astype(jnp.bfloat16)
            solved.append(level_partial)
            products = jnp.einsum("rsjab,rsbp->rsjap", blocks[:, first_row:end_row], level_partial.astype(jnp.float32))
            spread = jnp.zeros((N_ROW, SUB + TOP, B, RHS_DEV), jnp.float32)
            spread = spread.at[owner[:, first_row:end_row], codes[:, first_row:end_row]].add(products)
            acc_local = acc_local + spread[:, :SUB]
            acc_top = acc_top + jnp.sum(spread[:, SUB:], axis=0)
        top_values = []
        for step_index in range(TOP):
            carried = jnp.zeros((B, RHS_DEV), jnp.float32)
            for earlier in range(step_index):
                carried = carried + jnp.dot(top_factor[step_index, earlier], top_values[earlier], preferred_element_type=jnp.float32)
            residual_rows = ((top_panel[step_index].astype(jnp.float32) - acc_top[step_index]) - carried).astype(jnp.bfloat16)
            top_values.append(jnp.dot(top_inv[step_index], residual_rows, preferred_element_type=jnp.float32).astype(jnp.bfloat16))
        local_out = jnp.concatenate(solved, axis=1).reshape(NLOC, B, RHS_DEV)
        return local_out, jnp.stack(top_values)

    local_panels = local_rhs.reshape(NLOC, B, N_RHS, RHS_DEV).transpose(2, 0, 1, 3)
    top_panels = top_rhs.reshape(TOP, B, N_RHS, RHS_DEV).transpose(2, 0, 1, 3)
    local_out, top_out = lax.map(solve_panel, (local_panels, top_panels))
    local_solution = local_out.transpose(1, 2, 0, 3).reshape(NLOC, B, NRHS)
    top_solution = top_out.transpose(1, 2, 0, 3).reshape(TOP, B, NRHS)
    return local_solution, top_solution
```

```python
import jax
import jax.numpy as jnp
from jax import lax
from jax.experimental import pallas as pl
from jax.experimental.pallas import tpu as pltpu
from jax.sharding import PartitionSpec as P

SUB = 42
LEVELS = ((0, 24), (24, 36), (36, 42))
B = 128
NB = 4
TOP = 8
PARTS = 32
ROWS = B // PARTS
GROUP = 16
FIRST = LEVELS[0][1]
LATER = SUB - FIRST
LATER_PAD = -(-LATER // 4) * 4
LOW = tuple(k - k % 2 for k in range(TOP))
START = tuple(sum(TOP - LOW[q] for q in range(k)) for k in range(TOP))
TOP_BLOCKS = sum(TOP - low for low in LOW)
LEAD_ROWS = FIRST * (1 + NB) * ROWS
REST_ROWS = (LATER_PAD + LATER * NB + TOP_BLOCKS) * ROWS
DIAG_LATER = FIRST
DIAG_TOP = FIRST + LATER_PAD
W_BLOCKS = DIAG_TOP + TOP_BLOCKS
F32 = jnp.float32
BF16 = jnp.bfloat16


def substitute(
    codes, row, rhs, top_rhs, lead_hbm, rest_hbm, sol, part,
    lead, rest, stage, natural, weights, product, acc, base, sems,
):
    copies = (
        pltpu.make_async_copy(lead_hbm, lead, sems.at[0]),
        pltpu.make_async_copy(rest_hbm, rest, sems.at[1]),
    )
    for copy in copies:
        copy.start()
    acc[...] = jnp.zeros_like(acc)

    def collect(source, first_row, first_block, groups):
        def step(g, _):
            at = pl.multiple_of(first_row + g * GROUP, GROUP)
            rows = source[:, pl.ds(at, GROUP), :].astype(F32)
            stage[...] = rows.reshape(PARTS * GROUP, B)
            for q in range(GROUP // ROWS):
                for i in range(ROWS):
                    natural[q, pl.ds(i, PARTS, stride=ROWS), :] = stage[
                        pl.ds(q * ROWS + i, PARTS, stride=GROUP), :
                    ]
                weights[first_block + g * 4 + q] = natural[q].astype(BF16)
            return 0

        lax.fori_loop(0, groups, step, 0)

    def summed(target):
        for i in range(ROWS):
            natural[0, pl.ds(i, PARTS, stride=ROWS), :] = acc[target, pl.ds(i * PARTS, PARTS), :]
        return natural[0]

    def level(source, first, end, first_block, off_row, is_leaf):
        def step(n, _):
            s = first + n
            values = rhs[s]
            if not is_leaf:
                values = (values.astype(F32) - summed(s - FIRST)).astype(BF16)
            solved = jnp.dot(weights[first_block + n], values, preferred_element_type=F32)
            solved = solved.astype(BF16)
            sol[s] = solved
            at = pl.multiple_of(off_row + n * GROUP, GROUP)
            stacked = source[:, pl.ds(at, GROUP), :].reshape(PARTS * GROUP, B)
            slot = n % 2
            product[slot] = jnp.dot(stacked, solved, preferred_element_type=F32)
            for j in range(NB):
                target = codes[s * NB + j] - FIRST
                for i in range(ROWS):
                    into = pl.ds(i * PARTS, PARTS)
                    acc[target, into, :] += product[
                        slot, pl.ds(j * ROWS + i, PARTS, stride=GROUP), :
                    ]
            return 0

        lax.fori_loop(0, end - first, step, 0, unroll=2)

    copies[0].wait()
    collect(lead, 0, 0, FIRST // 4)
    level(lead, 0, FIRST, 0, FIRST * ROWS, True)
    copies[1].wait()
    collect(rest, 0, DIAG_LATER, LATER_PAD // 4)
    top_row = (LATER_PAD + LATER * NB) * ROWS
    collect(rest, top_row, DIAG_TOP, TOP_BLOCKS // 4)
    for first, end in LEVELS[1:]:
        off_row = LATER_PAD * ROWS + (first - FIRST) * GROUP
        level(rest, first, end, DIAG_LATER + first - FIRST, off_row, False)

    for t in range(TOP):
        own = jnp.where(row[0] == t, top_rhs[...].astype(F32), 0.0)
        base[t] = own - summed(SUB - FIRST + t)
    for k in range(TOP):
        at = DIAG_TOP + START[k] - LOW[k]
        solved = jnp.dot(weights[at + k], base[k].astype(BF16), preferred_element_type=F32)
        solved = solved.astype(BF16)
        part[k] = solved
        if k + 1 < TOP:
            below = weights[at + k + 1 : at + TOP].reshape((TOP - 1 - k) * B, B)
            update = jnp.dot(below, solved, preferred_element_type=F32)
            base[k + 1 :] = base[k + 1 :] - update.reshape(TOP - 1 - k, B, B)


def run_levels(codes, row, rhs, top_rhs, lead, rest):
    vmem = pl.BlockSpec(memory_space=pltpu.VMEM)
    smem = pl.BlockSpec(memory_space=pltpu.SMEM)
    hbm = pl.BlockSpec(memory_space=pl.ANY)
    flops = 2 * B**3 * (SUB * (1 + NB) + TOP * (TOP + 1) // 2)
    return pl.pallas_call(
        substitute,
        out_shape=(
            jax.ShapeDtypeStruct((SUB, B, B), BF16),
            jax.ShapeDtypeStruct((TOP, B, B), BF16),
        ),
        in_specs=[smem, smem, vmem, vmem, hbm, hbm],
        out_specs=(vmem, vmem),
        scratch_shapes=[
            pltpu.VMEM((PARTS, LEAD_ROWS, B), BF16),
            pltpu.VMEM((PARTS, REST_ROWS, B), BF16),
            pltpu.VMEM((PARTS * GROUP, B), F32),
            pltpu.VMEM((4, B, B), F32),
            pltpu.VMEM((W_BLOCKS, B, B), BF16),
            pltpu.VMEM((2, PARTS * GROUP, B), F32),
            pltpu.VMEM((SUB - FIRST + TOP, B, B), F32),
            pltpu.VMEM((TOP, B, B), F32),
            pltpu.SemaphoreType.DMA((2,)),
        ],
        compiler_params=pltpu.CompilerParams(vmem_limit_bytes=40 << 20),
        cost_estimate=pl.CostEstimate(flops=flops, bytes_accessed=12 << 20, transcendentals=0),
    )(codes, row, rhs, top_rhs, lead, rest)


def local(local_rhs, top_rhs, diag_inv, top_inv, off_blocks, top_factor, targets):
    position = lax.axis_index("row")
    own = (jnp.arange(TOP) == position)[:, None, None]
    top_rows = jnp.where(own, top_inv, top_factor[0])
    top_all = lax.all_gather(top_rows, "row", axis=0)
    top_rows = jnp.concatenate([top_all[LOW[k] :, k] for k in range(TOP)], axis=0)
    pad = jnp.zeros(((LATER_PAD - LATER) * ROWS, B), BF16)
    packed = jnp.concatenate(
        [
            diag_inv[:FIRST].reshape(-1, B),
            off_blocks[:FIRST].reshape(-1, B),
            diag_inv[FIRST:].reshape(-1, B),
            pad,
            off_blocks[FIRST:].reshape(-1, B),
            top_rows.reshape(-1, B),
        ],
        axis=0,
    )
    gathered = lax.all_gather(packed, "rhs", axis=0)
    solved, part = run_levels(
        targets.reshape(-1), position[None], local_rhs, top_rhs[0],
        gathered[:, :LEAD_ROWS], gathered[:, LEAD_ROWS:],
    )
    parts = lax.all_to_all(part, "row", 0, 0, tiled=True)
    own_top = jnp.sum(parts.astype(F32), axis=0, keepdims=True).astype(BF16)
    return solved, own_top


def solution(mesh):
    in_specs = (
        P("row", None, "rhs"),
        P("row", None, "rhs"),
        P("row", "rhs", None),
        P("row", "rhs", None),
        P("row", None, "rhs", None),
        P("row", None, "rhs", None),
        P("row", None),
    )
    out_specs = (P("row", None, "rhs"), P("row", None, "rhs"))
    return jax.shard_map(local, mesh=mesh, in_specs=in_specs, out_specs=out_specs, check_vma=False)
```

```python
import jax
import jax.numpy as jnp
from jax import lax
from jax.experimental import pallas as pl
from jax.experimental.pallas import tpu as pltpu
from jax.sharding import PartitionSpec as P

SUB = 42
LEVELS = ((0, 24), (24, 36), (36, 42))
B = 128
NB = 4
TOP = 8
PARTS = 32
ROWS = B // PARTS
GROUP = 16
FIRST = LEVELS[0][1]
LATER = SUB - FIRST
LATER_PAD = -(-LATER // 4) * 4
LOW = tuple(k - k % 2 for k in range(TOP))
START = tuple(sum(TOP - LOW[q] for q in range(k)) for k in range(TOP))
TOP_BLOCKS = sum(TOP - low for low in LOW)
LEAD_ROWS = FIRST * (1 + NB) * ROWS
REST_ROWS = (LATER_PAD + LATER * NB + TOP_BLOCKS) * ROWS
TOP_ROW = (LATER_PAD + LATER * NB) * ROWS
NY, NZ = 4, 8
Z_ORDER = (0, 1, -1, 2, -2, 3, -3, 4)
F32 = jnp.float32
BF16 = jnp.bfloat16


def collect(source, stage, natural, weights, first_row, first_block, groups):
    def step(g, _):
        at = pl.multiple_of(first_row + g * GROUP, GROUP)
        rows = source[:, pl.ds(at, GROUP), :].astype(F32)
        stage[...] = rows.reshape(PARTS * GROUP, B)
        for q in range(GROUP // ROWS):
            for i in range(ROWS):
                natural[q, pl.ds(i, PARTS, stride=ROWS), :] = stage[
                    pl.ds(q * ROWS + i, PARTS, stride=GROUP), :
                ]
            weights[first_block + g * 4 + q] = natural[q].astype(BF16)
        return 0

    lax.fori_loop(0, groups, step, 0)


def summed(acc, natural, target):
    for i in range(ROWS):
        natural[0, pl.ds(i, PARTS, stride=ROWS), :] = acc[target, pl.ds(i * PARTS, PARTS), :]
    return natural[0]


def solve_level(
    codes, rhs, source, weights, product, acc, natural, sol,
    first, end, shift, first_block, off_row, is_leaf,
):
    def step(n, _):
        s = first + n
        values = rhs[s - shift]
        if not is_leaf:
            values = (values.astype(F32) - summed(acc, natural, s - FIRST)).astype(BF16)
        solved = jnp.dot(weights[first_block + n], values, preferred_element_type=F32)
        solved = solved.astype(BF16)
        sol[s - shift] = solved
        at = pl.multiple_of(off_row + n * GROUP, GROUP)
        stacked = source[:, pl.ds(at, GROUP), :].reshape(PARTS * GROUP, B)
        slot = n % 2
        product[slot] = jnp.dot(stacked, solved, preferred_element_type=F32)
        for j in range(NB):
            target = codes[s * NB + j] - FIRST
            for i in range(ROWS):
                into = pl.ds(i * PARTS, PARTS)
                acc[target, into, :] += product[
                    slot, pl.ds(j * ROWS + i, PARTS, stride=GROUP), :
                ]
        return 0

    lax.fori_loop(0, end - first, step, 0, unroll=2)


def place(pieces, gathered, place_row, sems):
    copies = []
    for n, (ref, slot, dy, dz) in enumerate(pieces):
        part = lax.rem(place_row[1] - dy + NY, NY) * NZ + lax.rem(place_row[2] - dz + NZ, NZ)
        copies.append(pltpu.make_async_copy(ref.at[slot], gathered.at[part], sems.at[n]))
    for copy in copies:
        copy.start()
    return copies


def lead_pieces(own, right, left, far_low, far_high):
    half = NZ // 2
    pieces = []
    for q, dz in enumerate(Z_ORDER):
        pieces += [(own, q, 0, dz), (right, q, 1, dz), (left, q, -1, dz)]
        pieces.append((far_low, q, 2, dz) if q < half else (far_high, q - half, 2, dz))
    return pieces


def rest_pieces(near, far_low, far_high):
    pieces = []
    for q, dy in enumerate((0, 1, -1, 2)):
        pieces += [(ref, q, dy, Z_ORDER[m]) for m, ref in enumerate(near)]
        pieces.append((far_low, q, dy, 4) if q < 2 else (far_high, q - 2, dy, 4))
    return pieces


def leaf_level(
    codes, where, rhs, own, right, left, far_low, far_high, sol, acc_out,
    lead, stage, natural, weights, product, sems,
):
    copies = place(lead_pieces(own, right, left, far_low, far_high), lead, where, sems)
    acc_out[...] = jnp.zeros_like(acc_out)
    for copy in copies:
        copy.wait()
    collect(lead, stage, natural, weights, 0, 0, FIRST // 4)
    solve_level(
        codes, rhs, lead, weights, product, acc_out, natural, sol,
        0, FIRST, 0, 0, FIRST * ROWS, True,
    )


def later_levels(
    codes, where, rhs_hbm, top_rhs, acc_in, sol_in, n0, n1, n2, n3, n4, n5, n6, far_low, far_high,
    sol_hbm, part, rest, rhs, acc, sol, stage, natural, weights, product, base, sems, more_sems,
):
    del sol_in
    loads = (
        pltpu.make_async_copy(rhs_hbm.at[pl.ds(FIRST, LATER)], rhs, more_sems.at[0]),
        pltpu.make_async_copy(acc_in, acc, more_sems.at[1]),
    )
    for copy in loads:
        copy.start()
    pieces = rest_pieces((n0, n1, n2, n3, n4, n5, n6), far_low, far_high)
    for copy in place(pieces, rest, where, sems):
        copy.wait()
    collect(rest, stage, natural, weights, 0, 0, LATER_PAD // 4)
    collect(rest, stage, natural, weights, TOP_ROW, LATER_PAD, TOP_BLOCKS // 4)
    for copy in loads:
        copy.wait()
    for first, end in LEVELS[1:]:
        off_row = LATER_PAD * ROWS + (first - FIRST) * GROUP
        solve_level(
            codes, rhs, rest, weights, product, acc, natural, sol,
            first, end, FIRST, first - FIRST, off_row, False,
        )
    store = pltpu.make_async_copy(sol, sol_hbm.at[pl.ds(FIRST, LATER)], more_sems.at[2])
    store.start()

    for t in range(TOP):
        own = jnp.where(where[0] == t, top_rhs[...].astype(F32), 0.0)
        base[t] = own - summed(acc, natural, SUB - FIRST + t)
    for k in range(TOP):
        at = LATER_PAD + START[k] - LOW[k]
        solved = jnp.dot(weights[at + k], base[k].astype(BF16), preferred_element_type=F32)
        solved = solved.astype(BF16)
        part[k] = solved
        if k + 1 < TOP:
            below = weights[at + k + 1 : at + TOP].reshape((TOP - 1 - k) * B, B)
            update = jnp.dot(below, solved, preferred_element_type=F32)
            base[k + 1 :] = base[k + 1 :] - update.reshape(TOP - 1 - k, B, B)
    store.wait()


VMEM = pl.BlockSpec(memory_space=pltpu.VMEM)
SMEM = pl.BlockSpec(memory_space=pltpu.SMEM)
HBM = pl.BlockSpec(memory_space=pl.ANY)
WORK = (
    pltpu.VMEM((PARTS * GROUP, B), F32),
    pltpu.VMEM((4, B, B), F32),
)
ACC_SHAPE = (SUB - FIRST + TOP, B, B)


def cost(blocks, nbytes):
    return pl.CostEstimate(flops=2 * B**3 * blocks, bytes_accessed=nbytes, transcendentals=0)


def run_leaves(codes, where, rhs, pieces):
    block = pl.BlockSpec((FIRST, B, B), lambda n: (0, 0, 0))
    return pl.pallas_call(
        leaf_level,
        grid=(1,),
        out_shape=(
            jax.ShapeDtypeStruct((SUB, B, B), BF16),
            jax.ShapeDtypeStruct(ACC_SHAPE, F32),
        ),
        in_specs=[SMEM, SMEM, block] + [HBM] * 5,
        out_specs=(block, pl.BlockSpec(ACC_SHAPE, lambda n: (0, 0, 0))),
        scratch_shapes=[
            pltpu.VMEM((PARTS, LEAD_ROWS, B), BF16),
            *WORK,
            pltpu.VMEM((FIRST, B, B), BF16),
            pltpu.VMEM((2, PARTS * GROUP, B), F32),
            pltpu.SemaphoreType.DMA((PARTS,)),
        ],
        compiler_params=pltpu.CompilerParams(vmem_limit_bytes=32 << 20),
        cost_estimate=cost(FIRST * (1 + NB), 8 << 20),
    )(codes, where, rhs, *pieces)


def run_later(codes, where, rhs, top_rhs, acc, sol, pieces):
    return pl.pallas_call(
        later_levels,
        out_shape=(
            jax.ShapeDtypeStruct((SUB, B, B), BF16),
            jax.ShapeDtypeStruct((TOP, B, B), BF16),
        ),
        in_specs=[SMEM, SMEM, HBM, VMEM, HBM, HBM] + [HBM] * 9,
        out_specs=(HBM, VMEM),
        input_output_aliases={5: 0},
        scratch_shapes=[
            pltpu.VMEM((PARTS, REST_ROWS, B), BF16),
            pltpu.VMEM((LATER, B, B), BF16),
            pltpu.VMEM(ACC_SHAPE, F32),
            pltpu.VMEM((LATER, B, B), BF16),
            *WORK,
            pltpu.VMEM((LATER_PAD + TOP_BLOCKS, B, B), BF16),
            pltpu.VMEM((2, PARTS * GROUP, B), F32),
            pltpu.VMEM((TOP, B, B), F32),
            pltpu.SemaphoreType.DMA((PARTS,)),
            pltpu.SemaphoreType.DMA((3,)),
        ],
        compiler_params=pltpu.CompilerParams(vmem_limit_bytes=32 << 20),
        cost_estimate=cost(LATER * (1 + NB) + TOP * (TOP + 1) // 2, 8 << 20),
    )(codes, where, rhs, top_rhs, acc, sol, *pieces)


def shift_z(x, k):
    pairs = [(y * NZ + z, y * NZ + (z + k) % NZ) for y in range(NY) for z in range(NZ)]
    return lax.ppermute(x, "rhs", pairs)


def shift_y(x, k):
    pairs = [(y * NZ + z, (y + k) % NY * NZ + z) for y in range(NY) for z in range(NZ)]
    return lax.ppermute(x, "rhs", pairs)


def gather_z_then_y(x):
    held, right, left = [x], x, x
    for _ in range(3):
        right, left = shift_z(right, 1), shift_z(left, -1)
        held += [right, left]
    held.append(shift_z(right, 1))
    own = jnp.stack(held)
    right, left = shift_y(own, 1), shift_y(own, -1)
    half = NZ // 2
    return own, right, left, shift_y(right[:half], 1), shift_y(left[half:], -1)


def gather_y_then_z(x):
    own = jnp.stack([x, shift_y(x, 1), shift_y(x, -1), shift_y(x, 2)])
    held, right, left = [own], own, own
    for _ in range(3):
        right, left = shift_z(right, 1), shift_z(left, -1)
        held += [right, left]
    return (*held, shift_z(right[:2], 1), shift_z(left[2:], -1))


def local(local_rhs, top_rhs, diag_inv, top_inv, off_blocks, top_factor, targets):
    position, part = lax.axis_index("row"), lax.axis_index("rhs")
    own = (jnp.arange(TOP) == position)[:, None, None]
    top_rows = jnp.where(own, top_inv, top_factor[0])
    lead = jnp.concatenate(
        [diag_inv[:FIRST].reshape(-1, B), off_blocks[:FIRST].reshape(-1, B)], axis=0
    )
    lead_all = gather_z_then_y(lead)
    top_all = lax.all_gather(top_rows, "row", axis=0)
    top_rows = jnp.concatenate([top_all[LOW[k] :, k] for k in range(TOP)], axis=0)
    rest = jnp.concatenate(
        [
            diag_inv[FIRST:].reshape(-1, B),
            jnp.zeros(((LATER_PAD - LATER) * ROWS, B), BF16),
            off_blocks[FIRST:].reshape(-1, B),
            top_rows.reshape(-1, B),
        ],
        axis=0,
    )
    rest_all = gather_y_then_z(rest)
    codes = targets.reshape(-1)
    where = jnp.stack([position, part // NZ, part % NZ])
    sol, acc = run_leaves(codes, where, local_rhs, lead_all)
    sol, addends = run_later(codes, where, local_rhs, top_rhs[0], acc, sol, rest_all)
    parts = lax.all_to_all(addends, "row", 0, 0, tiled=True)
    own_top = jnp.sum(parts.astype(F32), axis=0, keepdims=True).astype(BF16)
    return sol, own_top


def solution(mesh):
    in_specs = (
        P("row", None, "rhs"),
        P("row", None, "rhs"),
        P("row", "rhs", None),
        P("row", "rhs", None),
        P("row", None, "rhs", None),
        P("row", None, "rhs", None),
        P("row", None),
    )
    out_specs = (P("row", None, "rhs"), P("row", None, "rhs"))
    return jax.shard_map(local, mesh=mesh, in_specs=in_specs, out_specs=out_specs, check_vma=False)
```

```python
import jax
import jax.numpy as jnp
from jax import lax
from jax.experimental import pallas as pl
from jax.experimental.pallas import tpu as pltpu
from jax.sharding import PartitionSpec as P

SUB = 42
LEVELS = ((0, 24), (24, 36), (36, 42))
B = 128
NB = 4
TOP = 8
PARTS = 32
ROWS = B // PARTS
GROUP = 16
FIRST = LEVELS[0][1]
LATER = SUB - FIRST
LATER_PAD = -(-LATER // 4) * 4
LOW = tuple(k - k % 2 for k in range(TOP))
START = tuple(sum(TOP - LOW[q] for q in range(k)) for k in range(TOP))
TOP_BLOCKS = sum(TOP - low for low in LOW)
LEAD_ROWS = FIRST * (1 + NB) * ROWS
REST_ROWS = (LATER_PAD + LATER * NB + TOP_BLOCKS) * ROWS
TOP_ROW = (LATER_PAD + LATER * NB) * ROWS
NY, NZ = 4, 8
ROW, RHS = ("x", "core"), ("y", "z")
F32 = jnp.float32
BF16 = jnp.bfloat16


def collect(source, stage, natural, weights, first_row, first_block, groups):
    def step(g, _):
        at = pl.multiple_of(first_row + g * GROUP, GROUP)
        rows = source[:, pl.ds(at, GROUP), :].astype(F32)
        stage[...] = rows.reshape(PARTS * GROUP, B)
        for q in range(GROUP // ROWS):
            for i in range(ROWS):
                natural[q, pl.ds(i, PARTS, stride=ROWS), :] = stage[
                    pl.ds(q * ROWS + i, PARTS, stride=GROUP), :
                ]
            weights[first_block + g * 4 + q] = natural[q].astype(BF16)
        return 0

    lax.fori_loop(0, groups, step, 0)


def summed(acc, natural, target):
    for i in range(ROWS):
        natural[0, pl.ds(i, PARTS, stride=ROWS), :] = acc[target, pl.ds(i * PARTS, PARTS), :]
    return natural[0]


def solve_level(
    codes, rhs, source, weights, product, acc, natural, sol,
    first, end, shift, first_block, off_row, is_leaf,
):
    for n in range(end - first):
        values = rhs[first + n]
        if not is_leaf:
            values = (values.astype(F32) - summed(acc, natural, first + n - FIRST)).astype(BF16)
        solved = jnp.dot(weights[first_block + n], values, preferred_element_type=F32)
        sol[first + n - shift] = solved.astype(BF16)
    for n in range(end - first):
        stacked = source[:, pl.ds(off_row + n * GROUP, GROUP), :].reshape(PARTS * GROUP, B)
        slot = n % 2
        product[slot] = jnp.dot(stacked, sol[first + n - shift], preferred_element_type=F32)
        for j in range(NB):
            target = codes[(first + n) * NB + j] - FIRST
            for i in range(ROWS):
                into = pl.ds(i * PARTS, PARTS)
                acc[target, into, :] += product[
                    slot, pl.ds(j * ROWS + i, PARTS, stride=GROUP), :
                ]


def leaf_level(codes, rhs, lead, sol, acc, stage, natural, weights, product):
    acc[...] = jnp.zeros_like(acc)
    collect(lead, stage, natural, weights, 0, 0, FIRST // 4)
    solve_level(
        codes, rhs, lead, weights, product, acc, natural, sol,
        0, FIRST, 0, 0, FIRST * ROWS, True,
    )


def later_levels(
    codes, where, rhs, top_rhs, acc_in, leaf_sol, rest,
    sol_hbm, part, acc, sol, stage, natural, weights, product, base, sems,
):
    stores = (
        pltpu.make_async_copy(leaf_sol, sol_hbm.at[pl.ds(0, FIRST)], sems.at[0]),
        pltpu.make_async_copy(sol, sol_hbm.at[pl.ds(FIRST, LATER)], sems.at[1]),
    )
    stores[0].start()
    acc[...] = acc_in[...]
    collect(rest, stage, natural, weights, 0, 0, LATER_PAD // 4)
    collect(rest, stage, natural, weights, TOP_ROW, LATER_PAD, TOP_BLOCKS // 4)
    for first, end in LEVELS[1:]:
        off_row = LATER_PAD * ROWS + (first - FIRST) * GROUP
        solve_level(
            codes, rhs, rest, weights, product, acc, natural, sol,
            first, end, FIRST, first - FIRST, off_row, False,
        )
    stores[1].start()

    for t in range(TOP):
        own = jnp.where(where[0] == t, top_rhs[...].astype(F32), 0.0)
        base[t] = own - summed(acc, natural, SUB - FIRST + t)
    for k in range(TOP):
        at = LATER_PAD + START[k] - LOW[k]
        solved = jnp.dot(weights[at + k], base[k].astype(BF16), preferred_element_type=F32)
        solved = solved.astype(BF16)
        part[k] = solved
        if k + 1 < TOP:
            below = weights[at + k + 1 : at + TOP].reshape((TOP - 1 - k) * B, B)
            update = jnp.dot(below, solved, preferred_element_type=F32)
            base[k + 1 :] = base[k + 1 :] - update.reshape(TOP - 1 - k, B, B)
    for store in stores:
        store.wait()


VMEM = pl.BlockSpec(memory_space=pltpu.VMEM)
SMEM = pl.BlockSpec(memory_space=pltpu.SMEM)
HBM = pl.BlockSpec(memory_space=pl.ANY)
WORK = (
    pltpu.VMEM((PARTS * GROUP, B), F32),
    pltpu.VMEM((4, B, B), F32),
)
ACC_SHAPE = (SUB - FIRST + TOP, B, B)


def cost(blocks, nbytes):
    return pl.CostEstimate(flops=2 * B**3 * blocks, bytes_accessed=nbytes, transcendentals=0)


def run_leaves(codes, rhs, lead):
    return pl.pallas_call(
        leaf_level,
        out_shape=(
            jax.ShapeDtypeStruct((FIRST, B, B), BF16),
            jax.ShapeDtypeStruct(ACC_SHAPE, F32),
        ),
        in_specs=[SMEM, VMEM, VMEM],
        out_specs=(VMEM, VMEM),
        scratch_shapes=[
            *WORK,
            pltpu.VMEM((FIRST, B, B), BF16),
            pltpu.VMEM((2, PARTS * GROUP, B), F32),
        ],
        compiler_params=pltpu.CompilerParams(vmem_limit_bytes=16 << 20),
        cost_estimate=cost(FIRST * (1 + NB), 8 << 20),
    )(codes, rhs, lead)


def run_later(codes, where, rhs, top_rhs, acc, leaf_sol, rest):
    return pl.pallas_call(
        later_levels,
        out_shape=(
            jax.ShapeDtypeStruct((SUB, B, B), BF16),
            jax.ShapeDtypeStruct((TOP, B, B), BF16),
        ),
        in_specs=[SMEM, SMEM] + [VMEM] * 5,
        out_specs=(HBM, VMEM),
        scratch_shapes=[
            pltpu.VMEM(ACC_SHAPE, F32),
            pltpu.VMEM((LATER, B, B), BF16),
            *WORK,
            pltpu.VMEM((LATER_PAD + TOP_BLOCKS, B, B), BF16),
            pltpu.VMEM((2, PARTS * GROUP, B), F32),
            pltpu.VMEM((TOP, B, B), F32),
            pltpu.SemaphoreType.DMA((2,)),
        ],
        compiler_params=pltpu.CompilerParams(vmem_limit_bytes=16 << 20),
        cost_estimate=cost(LATER * (1 + NB) + TOP * (TOP + 1) // 2, 8 << 20),
    )(codes, where, rhs, top_rhs, acc, leaf_sol, rest)


def shift(x, axis, k):
    size = lax.axis_size(axis)
    return lax.ppermute(x, axis, [(n, (n + k) % size) for n in range(size)])


def put(buffer, x, *start):
    start = start + (0,) * (buffer.ndim - len(start))
    shape = (1,) * (buffer.ndim - x.ndim) + x.shape
    return lax.dynamic_update_slice(buffer, x.reshape(shape), start)


def gather_z_then_y(x):
    y, z = lax.axis_index("y"), lax.axis_index("z")
    own = put(jnp.zeros((NZ, *x.shape), x.dtype), x, z)
    right, left = x, x
    for k in range(1, 4):
        right, left = shift(right, "z", 1), shift(left, "z", -1)
        own = put(put(own, right, (z - k) % NZ), left, (z + k) % NZ)
    own = put(own, shift(right, "z", 1), (z + 4) % NZ)
    half = NZ // 2
    every = put(jnp.zeros((NY, *own.shape), x.dtype), own, y)
    right, left = shift(own, "y", 1), shift(own, "y", -1)
    every = put(put(every, right, (y - 1) % NY), left, (y + 1) % NY)
    every = put(every, shift(right[:half], "y", 1)[None], (y + 2) % NY)
    every = put(every, shift(left[half:], "y", -1)[None], (y + 2) % NY, half)
    return every.reshape(PARTS, *x.shape)


def gather_y_then_z(x):
    y, z = lax.axis_index("y"), lax.axis_index("z")
    own = put(jnp.zeros((NY, *x.shape), x.dtype), x, y)
    for k in (1, -1, 2):
        own = put(own, shift(x, "y", k), (y - k) % NY)
    half = NY // 2
    every = put(jnp.zeros((NY, NZ, *x.shape), x.dtype), own[:, None], 0, z)
    right, left = own, own
    for k in range(1, 4):
        right, left = shift(right, "z", 1), shift(left, "z", -1)
        every = put(put(every, right[:, None], 0, (z - k) % NZ), left[:, None], 0, (z + k) % NZ)
    every = put(every, shift(right[:half], "z", 1)[:, None], 0, (z + 4) % NZ)
    every = put(every, shift(left[half:], "z", -1)[:, None], half, (z + 4) % NZ)
    return every.reshape(PARTS, *x.shape)


def gather_row(x):
    chip = lax.axis_index("x")
    pair = lax.all_gather(x, "core", axis=0)
    every = put(jnp.zeros((lax.axis_size("x"), *pair.shape), x.dtype), pair, chip)
    for k in (1, -1, 2):
        every = put(every, shift(pair, "x", k), (chip - k) % lax.axis_size("x"))
    return every.reshape(TOP, *x.shape)


def local(local_rhs, top_rhs, diag_inv, top_inv, off_blocks, top_factor, targets):
    position = lax.axis_index(ROW)
    diag, off = diag_inv.reshape(-1, B), off_blocks.reshape(-1, B)
    own = (jnp.arange(TOP) == position)[:, None, None]
    top_all = gather_row(jnp.where(own, top_inv, top_factor[0]))
    top_rows = jnp.concatenate([top_all[LOW[k] :, k] for k in range(TOP)], axis=0)
    lead = jnp.concatenate([diag[: FIRST * ROWS], off[: FIRST * GROUP]], axis=0)
    rest = jnp.concatenate(
        [
            diag[FIRST * ROWS :],
            jnp.zeros(((LATER_PAD - LATER) * ROWS, B), BF16),
            off[FIRST * GROUP :],
            top_rows.reshape(-1, B),
        ],
        axis=0,
    )
    lead_all = gather_z_then_y(lead)
    rest_all = gather_y_then_z(rest)
    codes = targets.reshape(-1)
    leaf_sol, acc = run_leaves(codes, local_rhs, lead_all)
    sol, addends = run_later(codes, position[None], local_rhs, top_rhs[0], acc, leaf_sol, rest_all)
    parts = lax.all_to_all(addends, ROW, 0, 0, tiled=True)
    own_top = jnp.sum(parts.astype(F32), axis=0, keepdims=True).astype(BF16)
    return sol, own_top


def solution(mesh):
    mesh = jax.sharding.Mesh(mesh.devices.reshape(4, 2, NY, NZ), (*ROW, *RHS))
    in_specs = (
        P(ROW, None, RHS),
        P(ROW, None, RHS),
        P(ROW, RHS, None),
        P(ROW, RHS, None),
        P(ROW, None, RHS, None),
        P(ROW, None, RHS, None),
        P(ROW, None),
    )
    out_specs = (P(ROW, None, RHS), P(ROW, None, RHS))
    return jax.shard_map(local, mesh=mesh, in_specs=in_specs, out_specs=out_specs, check_vma=False)
```

```python
import jax
import jax.numpy as jnp
from jax import lax
from jax.experimental import pallas as pl
from jax.experimental.pallas import tpu as pltpu
from jax.sharding import PartitionSpec as P

SUB = 42
LEVELS = ((0, 24), (24, 36), (36, 42))
B = 128
NB = 4
TOP = 8
PARTS = 32
ROWS = B // PARTS
GROUP = 16
FIRST = LEVELS[0][1]
LATER = SUB - FIRST
LATER_PAD = -(-LATER // 4) * 4
WIDTH = tuple(t - t % 2 + 2 for t in range(TOP))
START = tuple(sum(WIDTH[:t]) for t in range(TOP))
TOP_BLOCKS = sum(WIDTH)
LEAD_ROWS = FIRST * (1 + NB) * ROWS
REST_ROWS = (LATER_PAD + LATER * NB) * ROWS
TOP_ROWS = TOP * ROWS
ROW, RHS = ("x", "core"), ("y", "z")
NX, NY, NZ = 4, 4, 8
HI, LO = 2, 4
F32 = jnp.float32
BF16 = jnp.bfloat16


def collect(source, stage, natural, weights, first_row, first_block, groups):
    def step(g, _):
        at = pl.multiple_of(first_row + g * GROUP, GROUP)
        rows = source[:, pl.ds(at, GROUP), :].astype(F32)
        stage[...] = rows.reshape(PARTS * GROUP, B)
        for q in range(GROUP // ROWS):
            for i in range(ROWS):
                natural[q, pl.ds(i, PARTS, stride=ROWS), :] = stage[
                    pl.ds(q * ROWS + i, PARTS, stride=GROUP), :
                ]
            weights[first_block + g * 4 + q] = natural[q].astype(BF16)
        return 0

    lax.fori_loop(0, groups, step, 0)


def summed(acc, natural, target):
    for i in range(ROWS):
        natural[0, pl.ds(i, PARTS, stride=ROWS), :] = acc[target, pl.ds(i * PARTS, PARTS), :]
    return natural[0]


def solve_level(
    codes, rhs, source, weights, product, acc, natural, sol,
    first, end, shift, first_block, off_row, is_leaf,
):
    for n in range(end - first):
        values = rhs[first + n]
        if not is_leaf:
            values = (values.astype(F32) - summed(acc, natural, first + n - FIRST)).astype(BF16)
        solved = jnp.dot(weights[first_block + n], values, preferred_element_type=F32)
        sol[first + n - shift] = solved.astype(BF16)
    for n in range(end - first):
        stacked = source[:, pl.ds(off_row + n * GROUP, GROUP), :].reshape(PARTS * GROUP, B)
        slot = n % 2
        product[slot] = jnp.dot(stacked, sol[first + n - shift], preferred_element_type=F32)
        for j in range(NB):
            target = codes[(first + n) * NB + j] - FIRST
            for i in range(ROWS):
                into = pl.ds(i * PARTS, PARTS)
                acc[target, into, :] += product[
                    slot, pl.ds(j * ROWS + i, PARTS, stride=GROUP), :
                ]


def leaf_level(codes, rhs, lead, sol, acc, stage, natural, weights, product):
    acc[...] = jnp.zeros_like(acc)
    collect(lead, stage, natural, weights, 0, 0, FIRST // 4)
    solve_level(
        codes, rhs, lead, weights, product, acc, natural, sol,
        0, FIRST, 0, 0, FIRST * ROWS, True,
    )


def later_levels(
    codes, where, rhs, top_rhs, acc_in, leaf_sol, rest, top,
    sol_hbm, part, acc, sol, stage, natural, weights, product, base, sems,
):
    stores = (
        pltpu.make_async_copy(leaf_sol, sol_hbm.at[pl.ds(0, FIRST)], sems.at[0]),
        pltpu.make_async_copy(sol, sol_hbm.at[pl.ds(FIRST, LATER)], sems.at[1]),
    )
    stores[0].start()
    acc[...] = acc_in[...]
    collect(rest, stage, natural, weights, 0, 0, LATER_PAD // 4)
    collect(top, stage, natural, weights, 0, LATER_PAD, TOP_BLOCKS // 4)
    for first, end in LEVELS[1:]:
        off_row = LATER_PAD * ROWS + (first - FIRST) * GROUP
        solve_level(
            codes, rhs, rest, weights, product, acc, natural, sol,
            first, end, FIRST, first - FIRST, off_row, False,
        )
    stores[1].start()

    for t in range(TOP):
        own = jnp.where(where[0] == t, top_rhs[...].astype(F32), 0.0)
        base[t] = own - summed(acc, natural, SUB - FIRST + t)
    for k in range(TOP):
        at = LATER_PAD + k
        solved = jnp.dot(weights[at + START[k]], base[k].astype(BF16), preferred_element_type=F32)
        solved = solved.astype(BF16)
        part[k] = solved
        for t in range(k + 1, TOP):
            base[t] -= jnp.dot(weights[at + START[t]], solved, preferred_element_type=F32)
    for store in stores:
        store.wait()


VMEM = pl.BlockSpec(memory_space=pltpu.VMEM)
SMEM = pl.BlockSpec(memory_space=pltpu.SMEM)
HBM = pl.BlockSpec(memory_space=pl.ANY)
WORK = (
    pltpu.VMEM((PARTS * GROUP, B), F32),
    pltpu.VMEM((4, B, B), F32),
)
ACC_SHAPE = (SUB - FIRST + TOP, B, B)


def cost(blocks, nbytes):
    return pl.CostEstimate(flops=2 * B**3 * blocks, bytes_accessed=nbytes, transcendentals=0)


def run_leaves(codes, rhs, lead):
    return pl.pallas_call(
        leaf_level,
        out_shape=(
            jax.ShapeDtypeStruct((FIRST, B, B), BF16),
            jax.ShapeDtypeStruct(ACC_SHAPE, F32),
        ),
        in_specs=[SMEM, VMEM, VMEM],
        out_specs=(VMEM, VMEM),
        scratch_shapes=[
            *WORK,
            pltpu.VMEM((FIRST, B, B), BF16),
            pltpu.VMEM((2, PARTS * GROUP, B), F32),
        ],
        compiler_params=pltpu.CompilerParams(vmem_limit_bytes=16 << 20),
        cost_estimate=cost(FIRST * (1 + NB), 8 << 20),
    )(codes, rhs, lead)


def run_later(codes, where, rhs, top_rhs, acc, leaf_sol, rest, top):
    return pl.pallas_call(
        later_levels,
        out_shape=(
            jax.ShapeDtypeStruct((SUB, B, B), BF16),
            jax.ShapeDtypeStruct((TOP, B, B), BF16),
        ),
        in_specs=[SMEM, SMEM] + [VMEM] * 6,
        out_specs=(HBM, VMEM),
        scratch_shapes=[
            pltpu.VMEM(ACC_SHAPE, F32),
            pltpu.VMEM((LATER, B, B), BF16),
            *WORK,
            pltpu.VMEM((LATER_PAD + TOP_BLOCKS, B, B), BF16),
            pltpu.VMEM((2, PARTS * GROUP, B), F32),
            pltpu.VMEM((TOP, B, B), F32),
            pltpu.SemaphoreType.DMA((2,)),
        ],
        compiler_params=pltpu.CompilerParams(vmem_limit_bytes=16 << 20),
        cost_estimate=cost(LATER * (1 + NB) + TOP * (TOP + 1) // 2, 8 << 20),
    )(codes, where, rhs, top_rhs, acc, leaf_sol, rest, top)


def shift(x, axis, k):
    size = lax.axis_size(axis)
    return lax.ppermute(x, axis, [(n, (n + k) % size) for n in range(size)])


def put(buffer, x, *start):
    return lax.dynamic_update_slice(buffer, x, start + (0,) * (buffer.ndim - len(start)))


def gather(rows, top):
    chip, y, z = lax.axis_index("x"), lax.axis_index("y"), lax.axis_index("z")
    hi, lo = z // LO, z % LO
    packed = jnp.concatenate([rows, top], axis=0)
    other = shift(packed, "z", LO)
    pair = put(put(jnp.zeros((HI, *packed.shape), BF16), packed[None], hi), other[None], 1 - hi)
    lead, late = pair[:, :LEAD_ROWS], pair[:, LEAD_ROWS:]

    right, left = shift(lead, "z", 1), shift(lead, "z", -1)
    far_low, far_high = shift(right[:1], "z", 1), shift(left[1:], "z", -1)
    own = jnp.zeros((HI, LO, LEAD_ROWS, B), BF16)
    own = put(own, lead[:, None], 0, lo)
    own = put(own, right[:, None], 0, (lo - 1) % LO)
    own = put(own, left[:, None], 0, (lo + 1) % LO)
    own = put(own, far_low[:, None], 0, (lo + 2) % LO)
    own = put(own, far_high[:, None], 1, (lo + 2) % LO)

    late_all = put(jnp.zeros((NY, *late.shape), BF16), late[None], y)
    for k in (1, -1, 2):
        late_all = put(late_all, shift(late, "y", k)[None], (y - k) % NY)
    rest, top = late_all[:, :, :REST_ROWS], late_all[:, :, REST_ROWS:]
    rest_right, rest_left = shift(rest, "z", 1), shift(rest, "z", -1)

    right, left = shift(own, "y", 1), shift(own, "y", -1)

    cores = lax.all_gather(top, "core", axis=0)
    chips = put(jnp.zeros((NX, *cores.shape), BF16), cores[None], chip)
    for k in (1, -1, 2):
        chips = put(chips, shift(cores, "x", k)[None], (chip - k) % NX)
    chips = chips.reshape(TOP, NY, HI, TOP_ROWS, B)
    top = jnp.concatenate([chips[t, :, :, : WIDTH[t] * ROWS] for t in range(TOP)], axis=2)

    split = NY * REST_ROWS
    flat_top = top.reshape(-1, B)
    next_right = jnp.concatenate([rest_right[:, 0].reshape(-1, B), flat_top], axis=0)
    next_left = jnp.concatenate([rest_left[:, 1].reshape(-1, B), flat_top], axis=0)
    next_right, next_left = shift(next_right, "z", 1), shift(next_left, "z", -1)
    rest_low = next_right[:split].reshape(NY, 1, REST_ROWS, B)
    rest_high = next_left[:split].reshape(NY, 1, REST_ROWS, B)
    top_right, top_left = next_right[split:].reshape(top.shape), next_left[split:].reshape(top.shape)

    far_low, far_high = shift(right[:1], "y", 1), shift(left[1:], "y", -1)
    lead_all = put(jnp.zeros((NY, *own.shape), BF16), own[None], y)
    lead_all = put(lead_all, right[None], (y - 1) % NY)
    lead_all = put(lead_all, left[None], (y + 1) % NY)
    lead_all = put(lead_all, far_low[None], (y + 2) % NY)
    lead_all = put(lead_all, far_high[None], (y + 2) % NY, 1)

    top_low, top_high = shift(top_right[:, :1], "z", 1), shift(top_left[:, 1:], "z", -1)

    def join(own, right, left, low, high):
        every = jnp.zeros((NY, HI, LO, own.shape[2], B), BF16)
        every = put(every, own[:, :, None], 0, 0, lo)
        every = put(every, right[:, :, None], 0, 0, (lo - 1) % LO)
        every = put(every, left[:, :, None], 0, 0, (lo + 1) % LO)
        every = put(every, low[:, :, None], 0, 0, (lo + 2) % LO)
        every = put(every, high[:, :, None], 0, 1, (lo + 2) % LO)
        return every.reshape(PARTS, own.shape[2], B)

    rest_all = join(rest, rest_right, rest_left, rest_low, rest_high)
    top_all = join(top, top_right, top_left, top_low, top_high)
    return lead_all.reshape(PARTS, LEAD_ROWS, B), rest_all, top_all


def local(local_rhs, top_rhs, diag_inv, top_inv, off_blocks, top_factor, targets):
    position = lax.axis_index(ROW)
    diag, off = diag_inv.reshape(-1, B), off_blocks.reshape(-1, B)
    own = (jnp.arange(TOP) == position)[:, None, None]
    top_rows = jnp.where(own, top_inv, top_factor[0]).reshape(-1, B)
    pad = jnp.zeros(((LATER_PAD - LATER) * ROWS, B), BF16)
    rows = jnp.concatenate(
        [
            diag[: FIRST * ROWS],
            off[: FIRST * GROUP],
            diag[FIRST * ROWS :],
            pad,
            off[FIRST * GROUP :],
        ],
        axis=0,
    )
    lead_all, rest_all, top_all = gather(rows, top_rows)
    codes = targets.reshape(-1)
    leaf_sol, acc = run_leaves(codes, local_rhs, lead_all)
    sol, addends = run_later(
        codes, position[None], local_rhs, top_rhs[0], acc, leaf_sol, rest_all, top_all
    )
    parts = lax.all_to_all(addends, ROW, 0, 0, tiled=True)
    own_top = jnp.sum(parts.astype(F32), axis=0, keepdims=True).astype(BF16)
    return sol, own_top


def solution(mesh):
    mesh = jax.sharding.Mesh(mesh.devices.reshape(NX, 2, NY, NZ), (*ROW, *RHS))
    in_specs = (
        P(ROW, None, RHS),
        P(ROW, None, RHS),
        P(ROW, RHS, None),
        P(ROW, RHS, None),
        P(ROW, None, RHS, None),
        P(ROW, None, RHS, None),
        P(ROW, None),
    )
    out_specs = (P(ROW, None, RHS), P(ROW, None, RHS))
    return jax.shard_map(local, mesh=mesh, in_specs=in_specs, out_specs=out_specs, check_vma=False)
```

```python
import jax
import jax.numpy as jnp
from jax import lax
from jax.experimental import pallas as pl
from jax.experimental.pallas import tpu as pltpu
from jax.sharding import PartitionSpec as P

SUB = 42
LEVELS = ((0, 24), (24, 36), (36, 42))
B = 128
NB = 4
TOP = 8
PARTS = 32
ROWS = B // PARTS
GROUP = 16
FIRST = LEVELS[0][1]
LATER = SUB - FIRST
LATER_PAD = -(-LATER // 4) * 4
WIDTH = tuple(t - t % 2 + 2 for t in range(TOP))
START = tuple(sum(WIDTH[:t]) for t in range(TOP))
TOP_BLOCKS = sum(WIDTH)
LEAD_ROWS = FIRST * (1 + NB) * ROWS
REST_ROWS = (LATER_PAD + LATER * NB) * ROWS
TOP_ROWS = TOP * ROWS
ROW, RHS = ("x", "core"), ("y", "z")
NX, NY, NZ = 4, 4, 8
HI, LO = 2, 4
F32 = jnp.float32
BF16 = jnp.bfloat16


def collect(source, stage, natural, weights, first_row, first_block, groups):
    def step(g, _):
        at = pl.multiple_of(first_row + g * GROUP, GROUP)
        rows = source[:, pl.ds(at, GROUP), :].astype(F32)
        stage[...] = rows.reshape(PARTS * GROUP, B)
        for q in range(GROUP // ROWS):
            for i in range(ROWS):
                natural[q, pl.ds(i, PARTS, stride=ROWS), :] = stage[
                    pl.ds(q * ROWS + i, PARTS, stride=GROUP), :
                ]
            weights[first_block + g * 4 + q] = natural[q].astype(BF16)
        return 0

    lax.fori_loop(0, groups, step, 0)


def summed(acc, natural, target):
    for i in range(ROWS):
        natural[0, pl.ds(i, PARTS, stride=ROWS), :] = acc[target, pl.ds(i * PARTS, PARTS), :]
    return natural[0]


def solve_level(
    codes, rhs, source, weights, product, acc, natural, sol,
    first, end, shift, first_block, off_row, is_leaf,
):
    for n in range(end - first):
        values = rhs[first + n]
        if not is_leaf:
            values = (values.astype(F32) - summed(acc, natural, first + n - FIRST)).astype(BF16)
        solved = jnp.dot(weights[first_block + n], values, preferred_element_type=F32)
        sol[first + n - shift] = solved.astype(BF16)
    for n in range(end - first):
        stacked = source[:, pl.ds(off_row + n * GROUP, GROUP), :].reshape(PARTS * GROUP, B)
        slot = n % 2
        product[slot] = jnp.dot(stacked, sol[first + n - shift], preferred_element_type=F32)
        for j in range(NB):
            target = codes[(first + n) * NB + j] - FIRST
            for i in range(ROWS):
                into = pl.ds(i * PARTS, PARTS)
                acc[target, into, :] += product[
                    slot, pl.ds(j * ROWS + i, PARTS, stride=GROUP), :
                ]


def leaf_level(codes, rhs, lead, sol, acc, stage, natural, weights, product):
    acc[...] = jnp.zeros_like(acc)
    collect(lead, stage, natural, weights, 0, 0, FIRST // 4)
    solve_level(
        codes, rhs, lead, weights, product, acc, natural, sol,
        0, FIRST, 0, 0, FIRST * ROWS, True,
    )


def later_levels(
    codes, where, rhs, top_rhs, acc_in, leaf_sol, rest, top,
    sol_hbm, part, acc, sol, stage, natural, weights, product, base, sems,
):
    stores = (
        pltpu.make_async_copy(leaf_sol, sol_hbm.at[pl.ds(0, FIRST)], sems.at[0]),
        pltpu.make_async_copy(sol, sol_hbm.at[pl.ds(FIRST, LATER)], sems.at[1]),
    )
    stores[0].start()
    acc[...] = acc_in[...]
    collect(rest, stage, natural, weights, 0, 0, LATER_PAD // 4)
    collect(top, stage, natural, weights, 0, LATER_PAD, TOP_BLOCKS // 4)
    for first, end in LEVELS[1:]:
        off_row = LATER_PAD * ROWS + (first - FIRST) * GROUP
        solve_level(
            codes, rhs, rest, weights, product, acc, natural, sol,
            first, end, FIRST, first - FIRST, off_row, False,
        )
    stores[1].start()

    for t in range(TOP):
        own = jnp.where(where[0] == t, top_rhs[...].astype(F32), 0.0)
        base[t] = own - summed(acc, natural, SUB - FIRST + t)
    for k in range(TOP):
        at = LATER_PAD + k
        solved = jnp.dot(weights[at + START[k]], base[k].astype(BF16), preferred_element_type=F32)
        solved = solved.astype(BF16)
        part[k] = solved
        for t in range(k + 1, TOP):
            base[t] -= jnp.dot(weights[at + START[t]], solved, preferred_element_type=F32)
    for store in stores:
        store.wait()


def pack_rows(row, diag, off, factor, inverse, packed, factor_rows, inverse_rows, spread, sems):
    lead_diag, lead_off = FIRST * ROWS, FIRST * GROUP
    rest_diag, rest_off = LATER * ROWS, LATER * GROUP
    rest_at = LEAD_ROWS + LATER_PAD * ROWS
    copies = (
        pltpu.make_async_copy(factor, factor_rows, sems.at[0]),
        pltpu.make_async_copy(inverse, inverse_rows, sems.at[1]),
        pltpu.make_async_copy(diag.at[pl.ds(0, lead_diag)], packed.at[pl.ds(0, lead_diag)], sems.at[2]),
        pltpu.make_async_copy(off.at[pl.ds(0, lead_off)], packed.at[pl.ds(lead_diag, lead_off)], sems.at[3]),
        pltpu.make_async_copy(diag.at[pl.ds(lead_diag, rest_diag)], packed.at[pl.ds(LEAD_ROWS, rest_diag)], sems.at[4]),
        pltpu.make_async_copy(off.at[pl.ds(lead_off, rest_off)], packed.at[pl.ds(rest_at, rest_off)], sems.at[5]),
    )
    for copy in copies:
        copy.start()
    gap = (LATER_PAD - LATER) * ROWS
    packed[pl.ds(rest_at - gap, gap), :] = jnp.zeros((gap, B), BF16)
    copies[0].wait()
    copies[1].wait()
    for i in range(ROWS):
        line = inverse_rows[...].astype(F32)[i : i + 1]
        spread[pl.ds(i, TOP, stride=ROWS), :] = jnp.broadcast_to(line, (TOP, B))
    block = lax.broadcasted_iota(jnp.int32, (TOP_ROWS, B), 0) // ROWS
    top = jnp.where(block == row[0], spread[...], factor_rows[...].astype(F32))
    packed[pl.ds(LEAD_ROWS + REST_ROWS, TOP_ROWS), :] = top.astype(BF16)
    for copy in copies[2:]:
        copy.wait()


VMEM = pl.BlockSpec(memory_space=pltpu.VMEM)
SMEM = pl.BlockSpec(memory_space=pltpu.SMEM)
HBM = pl.BlockSpec(memory_space=pl.ANY)
WORK = (
    pltpu.VMEM((PARTS * GROUP, B), F32),
    pltpu.VMEM((4, B, B), F32),
)
ACC_SHAPE = (SUB - FIRST + TOP, B, B)


def cost(blocks, nbytes):
    return pl.CostEstimate(flops=2 * B**3 * blocks, bytes_accessed=nbytes, transcendentals=0)


def run_pack(row, diag, off, factor, inverse):
    return pl.pallas_call(
        pack_rows,
        out_shape=jax.ShapeDtypeStruct((LEAD_ROWS + REST_ROWS + TOP_ROWS, B), BF16),
        in_specs=[SMEM] + [HBM] * 4,
        out_specs=VMEM,
        scratch_shapes=[
            pltpu.VMEM((TOP_ROWS, B), BF16),
            pltpu.VMEM((ROWS, B), BF16),
            pltpu.VMEM((TOP_ROWS, B), F32),
            pltpu.SemaphoreType.DMA((6,)),
        ],
        compiler_params=pltpu.CompilerParams(vmem_limit_bytes=2 << 20),
        cost_estimate=cost(0, 1 << 19),
    )(row, diag, off, factor, inverse)


def run_leaves(codes, rhs, lead):
    return pl.pallas_call(
        leaf_level,
        out_shape=(
            jax.ShapeDtypeStruct((FIRST, B, B), BF16),
            jax.ShapeDtypeStruct(ACC_SHAPE, F32),
        ),
        in_specs=[SMEM, VMEM, VMEM],
        out_specs=(VMEM, VMEM),
        scratch_shapes=[
            *WORK,
            pltpu.VMEM((FIRST, B, B), BF16),
            pltpu.VMEM((2, PARTS * GROUP, B), F32),
        ],
        compiler_params=pltpu.CompilerParams(vmem_limit_bytes=16 << 20),
        cost_estimate=cost(FIRST * (1 + NB), 8 << 20),
    )(codes, rhs, lead)


def run_later(codes, where, rhs, top_rhs, acc, leaf_sol, rest, top):
    return pl.pallas_call(
        later_levels,
        out_shape=(
            jax.ShapeDtypeStruct((SUB, B, B), BF16),
            jax.ShapeDtypeStruct((TOP, B, B), BF16),
        ),
        in_specs=[SMEM, SMEM] + [VMEM] * 6,
        out_specs=(HBM, VMEM),
        scratch_shapes=[
            pltpu.VMEM(ACC_SHAPE, F32),
            pltpu.VMEM((LATER, B, B), BF16),
            *WORK,
            pltpu.VMEM((LATER_PAD + TOP_BLOCKS, B, B), BF16),
            pltpu.VMEM((2, PARTS * GROUP, B), F32),
            pltpu.VMEM((TOP, B, B), F32),
            pltpu.SemaphoreType.DMA((2,)),
        ],
        compiler_params=pltpu.CompilerParams(vmem_limit_bytes=16 << 20),
        cost_estimate=cost(LATER * (1 + NB) + TOP * (TOP + 1) // 2, 8 << 20),
    )(codes, where, rhs, top_rhs, acc, leaf_sol, rest, top)


def shift(x, axis, k):
    size = lax.axis_size(axis)
    return lax.ppermute(x, axis, [(n, (n + k) % size) for n in range(size)])


def put(buffer, x, *start):
    return lax.dynamic_update_slice(buffer, x, start + (0,) * (buffer.ndim - len(start)))


def gather(packed):
    chip, y, z = lax.axis_index("x"), lax.axis_index("y"), lax.axis_index("z")
    hi, lo = z // LO, z % LO
    other = shift(packed, "z", LO)
    pair = put(put(jnp.zeros((HI, *packed.shape), BF16), packed[None], hi), other[None], 1 - hi)
    lead, late = pair[:, :LEAD_ROWS], pair[:, LEAD_ROWS:]

    right, left = shift(lead, "z", 1), shift(lead, "z", -1)
    far_low, far_high = shift(right[:1], "z", 1), shift(left[1:], "z", -1)
    own = jnp.zeros((HI, LO, LEAD_ROWS, B), BF16)
    own = put(own, lead[:, None], 0, lo)
    own = put(own, right[:, None], 0, (lo - 1) % LO)
    own = put(own, left[:, None], 0, (lo + 1) % LO)
    own = put(own, far_low[:, None], 0, (lo + 2) % LO)
    own = put(own, far_high[:, None], 1, (lo + 2) % LO)

    late_all = put(jnp.zeros((NY, *late.shape), BF16), late[None], y)
    for k in (1, -1, 2):
        late_all = put(late_all, shift(late, "y", k)[None], (y - k) % NY)
    late_all, own = lax.optimization_barrier((late_all, own))
    rest, top = late_all[:, :, :REST_ROWS], late_all[:, :, REST_ROWS:]
    rest_right, rest_left = shift(rest, "z", 1), shift(rest, "z", -1)

    right, left = shift(own, "y", 1), shift(own, "y", -1)

    cores = lax.all_gather(top, "core", axis=0)
    chips = put(jnp.zeros((NX, *cores.shape), BF16), cores[None], chip)
    for k in (1, -1, 2):
        chips = put(chips, shift(cores, "x", k)[None], (chip - k) % NX)
    chips = chips.reshape(TOP, NY, HI, TOP_ROWS, B)
    top = jnp.concatenate([chips[t, :, :, : WIDTH[t] * ROWS] for t in range(TOP)], axis=2)

    split = NY * REST_ROWS
    flat_top = top.reshape(-1, B)
    next_right = jnp.concatenate([rest_right[:, 0].reshape(-1, B), flat_top], axis=0)
    next_left = jnp.concatenate([rest_left[:, 1].reshape(-1, B), flat_top], axis=0)
    next_right, next_left = shift(next_right, "z", 1), shift(next_left, "z", -1)
    rest_low = next_right[:split].reshape(NY, 1, REST_ROWS, B)
    rest_high = next_left[:split].reshape(NY, 1, REST_ROWS, B)
    top_right, top_left = next_right[split:].reshape(top.shape), next_left[split:].reshape(top.shape)

    far_low, far_high = shift(right[:1], "y", 1), shift(left[1:], "y", -1)
    lead_all = put(jnp.zeros((NY, *own.shape), BF16), own[None], y)
    lead_all = put(lead_all, right[None], (y - 1) % NY)
    lead_all = put(lead_all, left[None], (y + 1) % NY)
    lead_all = put(lead_all, far_low[None], (y + 2) % NY)
    lead_all = put(lead_all, far_high[None], (y + 2) % NY, 1)

    top_low, top_high = shift(top_right[:, :1], "z", 1), shift(top_left[:, 1:], "z", -1)

    def join(own, right, left, low, high):
        every = jnp.zeros((NY, HI, LO, own.shape[2], B), BF16)
        every = put(every, own[:, :, None], 0, 0, lo)
        every = put(every, right[:, :, None], 0, 0, (lo - 1) % LO)
        every = put(every, left[:, :, None], 0, 0, (lo + 1) % LO)
        every = put(every, low[:, :, None], 0, 0, (lo + 2) % LO)
        every = put(every, high[:, :, None], 0, 1, (lo + 2) % LO)
        return every.reshape(PARTS, own.shape[2], B)

    rest_all = join(rest, rest_right, rest_left, rest_low, rest_high)
    top_all = join(top, top_right, top_left, top_low, top_high)
    return lead_all.reshape(PARTS, LEAD_ROWS, B), rest_all, top_all


def local(local_rhs, top_rhs, diag_inv, top_inv, off_blocks, top_factor, targets):
    position = lax.axis_index(ROW)
    packed = run_pack(
        position[None],
        diag_inv.reshape(-1, B),
        off_blocks.reshape(-1, B),
        top_factor.reshape(-1, B),
        top_inv.reshape(-1, B),
    )
    lead_all, rest_all, top_all = gather(packed)
    codes = targets.reshape(-1)
    leaf_sol, acc = run_leaves(codes, local_rhs, lead_all)
    sol, addends = run_later(
        codes, position[None], local_rhs, top_rhs[0], acc, leaf_sol, rest_all, top_all
    )
    parts = lax.all_to_all(addends, ROW, 0, 0, tiled=True)
    own_top = jnp.sum(parts.astype(F32), axis=0, keepdims=True).astype(BF16)
    return sol, own_top


def solution(mesh):
    mesh = jax.sharding.Mesh(mesh.devices.reshape(NX, 2, NY, NZ), (*ROW, *RHS))
    in_specs = (
        P(ROW, None, RHS),
        P(ROW, None, RHS),
        P(ROW, RHS, None),
        P(ROW, RHS, None),
        P(ROW, None, RHS, None),
        P(ROW, None, RHS, None),
        P(ROW, None),
    )
    out_specs = (P(ROW, None, RHS), P(ROW, None, RHS))
    return jax.shard_map(local, mesh=mesh, in_specs=in_specs, out_specs=out_specs, check_vma=False)
```

```python
import jax
import jax.numpy as jnp
from jax import lax
from jax.experimental import pallas as pl
from jax.experimental.pallas import tpu as pltpu
from jax.sharding import PartitionSpec as P

SUB = 42
LEVELS = ((0, 24), (24, 36), (36, 42))
B = 128
NB = 4
TOP = 8
PARTS = 32
ROWS = B // PARTS
GROUP = 16
FIRST = LEVELS[0][1]
LATER = SUB - FIRST
LATER_PAD = -(-LATER // 4) * 4
WIDTH = tuple(t - t % 2 + 2 for t in range(TOP))
START = tuple(sum(WIDTH[:t]) for t in range(TOP))
TOP_BLOCKS = sum(WIDTH)
LEAD_ROWS = FIRST * (1 + NB) * ROWS
REST_ROWS = (LATER_PAD + LATER * NB + TOP_BLOCKS) * ROWS
TOP_ROW = (LATER_PAD + LATER * NB) * ROWS
NY, NZ = 4, 8
ROW, RHS = ("x", "core"), ("y", "z")
F32 = jnp.float32
BF16 = jnp.bfloat16


def collect(source, stage, natural, weights, first_row, first_block, groups):
    def step(g, _):
        at = pl.multiple_of(first_row + g * GROUP, GROUP)
        rows = source[:, pl.ds(at, GROUP), :].astype(F32)
        stage[...] = rows.reshape(PARTS * GROUP, B)
        for q in range(GROUP // ROWS):
            for i in range(ROWS):
                natural[q, pl.ds(i, PARTS, stride=ROWS), :] = stage[
                    pl.ds(q * ROWS + i, PARTS, stride=GROUP), :
                ]
            weights[first_block + g * 4 + q] = natural[q].astype(BF16)
        return 0

    lax.fori_loop(0, groups, step, 0)


def summed(acc, natural, target):
    for i in range(ROWS):
        natural[0, pl.ds(i, PARTS, stride=ROWS), :] = acc[target, pl.ds(i * PARTS, PARTS), :]
    return natural[0]


def solve_level(
    codes, rhs, source, weights, product, acc, natural, sol,
    first, end, shift, first_block, off_row, is_leaf,
):
    for n in range(end - first):
        values = rhs[first + n]
        if not is_leaf:
            values = (values.astype(F32) - summed(acc, natural, first + n - FIRST)).astype(BF16)
        solved = jnp.dot(weights[first_block + n], values, preferred_element_type=F32)
        sol[first + n - shift] = solved.astype(BF16)
    for n in range(end - first):
        stacked = source[:, pl.ds(off_row + n * GROUP, GROUP), :].reshape(PARTS * GROUP, B)
        slot = n % 2
        product[slot] = jnp.dot(stacked, sol[first + n - shift], preferred_element_type=F32)
        for j in range(NB):
            target = codes[(first + n) * NB + j] - FIRST
            for i in range(ROWS):
                into = pl.ds(i * PARTS, PARTS)
                acc[target, into, :] += product[
                    slot, pl.ds(j * ROWS + i, PARTS, stride=GROUP), :
                ]


def leaf_level(codes, rhs, lead, sol, acc, stage, natural, weights, product):
    acc[...] = jnp.zeros_like(acc)
    collect(lead, stage, natural, weights, 0, 0, FIRST // 4)
    solve_level(
        codes, rhs, lead, weights, product, acc, natural, sol,
        0, FIRST, 0, 0, FIRST * ROWS, True,
    )


def later_levels(
    codes, where, rhs, top_rhs, acc_in, leaf_sol, rest,
    sol_hbm, part, acc, sol, stage, natural, weights, product, base, sems,
):
    stores = (
        pltpu.make_async_copy(leaf_sol, sol_hbm.at[pl.ds(0, FIRST)], sems.at[0]),
        pltpu.make_async_copy(sol, sol_hbm.at[pl.ds(FIRST, LATER)], sems.at[1]),
    )
    stores[0].start()
    acc[...] = acc_in[...]
    collect(rest, stage, natural, weights, 0, 0, LATER_PAD // 4)
    collect(rest, stage, natural, weights, TOP_ROW, LATER_PAD, TOP_BLOCKS // 4)
    for first, end in LEVELS[1:]:
        off_row = LATER_PAD * ROWS + (first - FIRST) * GROUP
        solve_level(
            codes, rhs, rest, weights, product, acc, natural, sol,
            first, end, FIRST, first - FIRST, off_row, False,
        )
    stores[1].start()

    for t in range(TOP):
        own = jnp.where(where[0] == t, top_rhs[...].astype(F32), 0.0)
        base[t] = own - summed(acc, natural, SUB - FIRST + t)
    for k in range(TOP):
        at = LATER_PAD + k
        solved = jnp.dot(weights[at + START[k]], base[k].astype(BF16), preferred_element_type=F32)
        solved = solved.astype(BF16)
        part[k] = solved
        for t in range(k + 1, TOP):
            base[t] -= jnp.dot(weights[at + START[t]], solved, preferred_element_type=F32)
    for store in stores:
        store.wait()


def pack_rows(row, diag, off, factor, inverse, lead, rest, own, factor_rows, inverse_rows, spread, sems):
    lead_diag, lead_off = FIRST * ROWS, FIRST * GROUP
    rest_diag, rest_off = LATER * ROWS, LATER * GROUP
    rest_at = LATER_PAD * ROWS
    copies = (
        pltpu.make_async_copy(factor, factor_rows, sems.at[0]),
        pltpu.make_async_copy(inverse, inverse_rows, sems.at[1]),
        pltpu.make_async_copy(diag.at[pl.ds(0, lead_diag)], lead.at[pl.ds(0, lead_diag)], sems.at[2]),
        pltpu.make_async_copy(off.at[pl.ds(0, lead_off)], lead.at[pl.ds(lead_diag, lead_off)], sems.at[3]),
        pltpu.make_async_copy(diag.at[pl.ds(lead_diag, rest_diag)], rest.at[pl.ds(0, rest_diag)], sems.at[4]),
        pltpu.make_async_copy(off.at[pl.ds(lead_off, rest_off)], rest.at[pl.ds(rest_at, rest_off)], sems.at[5]),
    )
    for copy in copies:
        copy.start()
    gap = (LATER_PAD - LATER) * ROWS
    rest[pl.ds(rest_at - gap, gap), :] = jnp.zeros((gap, B), BF16)
    copies[0].wait()
    copies[1].wait()
    for i in range(ROWS):
        line = inverse_rows[...].astype(F32)[i : i + 1]
        spread[pl.ds(i, TOP, stride=ROWS), :] = jnp.broadcast_to(line, (TOP, B))
    block = lax.broadcasted_iota(jnp.int32, (TOP * ROWS, B), 0) // ROWS
    top = jnp.where(block == row[0], spread[...], factor_rows[...].astype(F32))
    own[...] = top.astype(BF16)
    for copy in copies[2:]:
        copy.wait()


VMEM = pl.BlockSpec(memory_space=pltpu.VMEM)
SMEM = pl.BlockSpec(memory_space=pltpu.SMEM)
HBM = pl.BlockSpec(memory_space=pl.ANY)
WORK = (
    pltpu.VMEM((PARTS * GROUP, B), F32),
    pltpu.VMEM((4, B, B), F32),
)
ACC_SHAPE = (SUB - FIRST + TOP, B, B)


def cost(blocks, nbytes):
    return pl.CostEstimate(flops=2 * B**3 * blocks, bytes_accessed=nbytes, transcendentals=0)


def run_pack(row, diag, off, factor, inverse):
    return pl.pallas_call(
        pack_rows,
        out_shape=[
            jax.ShapeDtypeStruct((rows, B), BF16) for rows in (LEAD_ROWS, TOP_ROW, TOP * ROWS)
        ],
        in_specs=[SMEM] + [HBM] * 4,
        out_specs=[VMEM] * 3,
        scratch_shapes=[
            pltpu.VMEM((TOP * ROWS, B), BF16),
            pltpu.VMEM((ROWS, B), BF16),
            pltpu.VMEM((TOP * ROWS, B), F32),
            pltpu.SemaphoreType.DMA((6,)),
        ],
        compiler_params=pltpu.CompilerParams(vmem_limit_bytes=56 << 20),
        cost_estimate=cost(0, 1 << 19),
    )(row, diag, off, factor, inverse)


def run_leaves(codes, rhs, lead):
    return pl.pallas_call(
        leaf_level,
        out_shape=(
            jax.ShapeDtypeStruct((FIRST, B, B), BF16),
            jax.ShapeDtypeStruct(ACC_SHAPE, F32),
        ),
        in_specs=[SMEM, VMEM, VMEM],
        out_specs=(VMEM, VMEM),
        scratch_shapes=[
            *WORK,
            pltpu.VMEM((FIRST, B, B), BF16),
            pltpu.VMEM((2, PARTS * GROUP, B), F32),
        ],
        compiler_params=pltpu.CompilerParams(vmem_limit_bytes=16 << 20),
        cost_estimate=cost(FIRST * (1 + NB), 8 << 20),
    )(codes, rhs, lead)


def run_later(codes, where, rhs, top_rhs, acc, leaf_sol, rest):
    return pl.pallas_call(
        later_levels,
        out_shape=(
            jax.ShapeDtypeStruct((SUB, B, B), BF16),
            jax.ShapeDtypeStruct((TOP, B, B), BF16),
        ),
        in_specs=[SMEM, SMEM] + [VMEM] * 5,
        out_specs=(HBM, VMEM),
        scratch_shapes=[
            pltpu.VMEM(ACC_SHAPE, F32),
            pltpu.VMEM((LATER, B, B), BF16),
            *WORK,
            pltpu.VMEM((LATER_PAD + TOP_BLOCKS, B, B), BF16),
            pltpu.VMEM((2, PARTS * GROUP, B), F32),
            pltpu.VMEM((TOP, B, B), F32),
            pltpu.SemaphoreType.DMA((2,)),
        ],
        compiler_params=pltpu.CompilerParams(vmem_limit_bytes=16 << 20),
        cost_estimate=cost(LATER * (1 + NB) + TOP * (TOP + 1) // 2, 8 << 20),
    )(codes, where, rhs, top_rhs, acc, leaf_sol, rest)


def shift(x, axis, k):
    size = lax.axis_size(axis)
    return lax.ppermute(x, axis, [(n, (n + k) % size) for n in range(size)])


def put(buffer, x, *start):
    start = start + (0,) * (buffer.ndim - len(start))
    shape = (1,) * (buffer.ndim - x.ndim) + x.shape
    return lax.dynamic_update_slice(buffer, x.reshape(shape), start)


def gather_z_then_y(x):
    y, z = lax.axis_index("y"), lax.axis_index("z")
    own = put(jnp.zeros((NZ, *x.shape), x.dtype), x, z)
    right, left = x, x
    for k in range(1, 4):
        right, left = shift(right, "z", 1), shift(left, "z", -1)
        own = put(put(own, right, (z - k) % NZ), left, (z + k) % NZ)
    own = put(own, shift(right, "z", 1), (z + 4) % NZ)
    half = NZ // 2
    every = put(jnp.zeros((NY, *own.shape), x.dtype), own, y)
    right, left = shift(own, "y", 1), shift(own, "y", -1)
    every = put(put(every, right, (y - 1) % NY), left, (y + 1) % NY)
    every = put(every, shift(right[:half], "y", 1)[None], (y + 2) % NY)
    every = put(every, shift(left[half:], "y", -1)[None], (y + 2) % NY, half)
    return every.reshape(PARTS, *x.shape)


def gather_y_then_z(x):
    y, z = lax.axis_index("y"), lax.axis_index("z")
    own = put(jnp.zeros((NY, *x.shape), x.dtype), x, y)
    for k in (1, -1, 2):
        own = put(own, shift(x, "y", k), (y - k) % NY)
    half = NY // 2
    every = put(jnp.zeros((NY, NZ, *x.shape), x.dtype), own[:, None], 0, z)
    right, left = own, own
    for k in range(1, 4):
        right, left = shift(right, "z", 1), shift(left, "z", -1)
        every = put(put(every, right[:, None], 0, (z - k) % NZ), left[:, None], 0, (z + k) % NZ)
    every = put(every, shift(right[:half], "z", 1)[:, None], 0, (z + 4) % NZ)
    every = put(every, shift(left[half:], "z", -1)[:, None], half, (z + 4) % NZ)
    return every.reshape(PARTS, *x.shape)


def gather_row(x):
    chip = lax.axis_index("x")
    pair = lax.all_gather(x, "core", axis=0)
    every = put(jnp.zeros((lax.axis_size("x"), *pair.shape), x.dtype), pair, chip)
    for k in (1, -1, 2):
        every = put(every, shift(pair, "x", k), (chip - k) % lax.axis_size("x"))
    return every.reshape(TOP, *x.shape)


def local(local_rhs, top_rhs, diag_inv, top_inv, off_blocks, top_factor, targets):
    position = lax.axis_index(ROW)
    lead, rest, top_rows = run_pack(
        position[None],
        diag_inv.reshape(-1, B),
        off_blocks.reshape(-1, B),
        top_factor.reshape(-1, B),
        top_inv.reshape(-1, B),
    )
    top_all = gather_row(top_rows)
    rest = jnp.concatenate([rest, *(top_all[t, : WIDTH[t] * ROWS] for t in range(TOP))], axis=0)
    lead_all = gather_z_then_y(lead)
    rest_all = gather_y_then_z(rest)
    codes = targets.reshape(-1)
    leaf_sol, acc = run_leaves(codes, local_rhs, lead_all)
    sol, addends = run_later(codes, position[None], local_rhs, top_rhs[0], acc, leaf_sol, rest_all)
    parts = lax.all_to_all(addends, ROW, 0, 0, tiled=True)
    own_top = jnp.sum(parts.astype(F32), axis=0, keepdims=True).astype(BF16)
    return sol, own_top


def solution(mesh):
    mesh = jax.sharding.Mesh(mesh.devices.reshape(4, 2, NY, NZ), (*ROW, *RHS))
    in_specs = (
        P(ROW, None, RHS),
        P(ROW, None, RHS),
        P(ROW, RHS, None),
        P(ROW, RHS, None),
        P(ROW, None, RHS, None),
        P(ROW, None, RHS, None),
        P(ROW, None),
    )
    out_specs = (P(ROW, None, RHS), P(ROW, None, RHS))
    return jax.shard_map(local, mesh=mesh, in_specs=in_specs, out_specs=out_specs, check_vma=False)
```

```python
import jax
import jax.numpy as jnp
from jax import lax
from jax.experimental import pallas as pl
from jax.experimental.pallas import tpu as pltpu
from jax.sharding import PartitionSpec as P

SUB = 42
LEVELS = ((0, 24), (24, 36), (36, 42))
B = 128
NB = 4
TOP = 8
PARTS = 32
ROWS = B // PARTS
GROUP = 16
FIRST = LEVELS[0][1]
LATER = SUB - FIRST
LATER_PAD = -(-LATER // 4) * 4
WIDTH = tuple(t - t % 2 + 2 for t in range(TOP))
START = tuple(sum(WIDTH[:t]) for t in range(TOP))
TOP_BLOCKS = sum(WIDTH)
LEAD_ROWS = FIRST * (1 + NB) * ROWS
REST_ROWS = (LATER_PAD + LATER * NB + TOP_BLOCKS) * ROWS
TOP_ROW = (LATER_PAD + LATER * NB) * ROWS
NY, NZ = 4, 8
ROW, RHS = ("x", "core"), ("y", "z")
F32 = jnp.float32
BF16 = jnp.bfloat16


def collect(source, stage, natural, weights, first_row, first_block, groups):
    def step(g, _):
        at = pl.multiple_of(first_row + g * GROUP, GROUP)
        rows = source[:, pl.ds(at, GROUP), :].astype(F32)
        stage[...] = rows.reshape(PARTS * GROUP, B)
        for q in range(GROUP // ROWS):
            for i in range(ROWS):
                natural[q, pl.ds(i, PARTS, stride=ROWS), :] = stage[
                    pl.ds(q * ROWS + i, PARTS, stride=GROUP), :
                ]
            weights[first_block + g * 4 + q] = natural[q].astype(BF16)
        return 0

    lax.fori_loop(0, groups, step, 0)


def summed(acc, natural, target):
    for i in range(ROWS):
        natural[0, pl.ds(i, PARTS, stride=ROWS), :] = acc[target, pl.ds(i * PARTS, PARTS), :]
    return natural[0]


def solve_level(
    codes, rhs, source, weights, product, acc, natural, sol,
    first, end, shift, first_block, off_row, is_leaf,
):
    for n in range(end - first):
        values = rhs[first + n]
        if not is_leaf:
            values = (values.astype(F32) - summed(acc, natural, first + n - FIRST)).astype(BF16)
        solved = jnp.dot(weights[first_block + n], values, preferred_element_type=F32)
        sol[first + n - shift] = solved.astype(BF16)
    for n in range(end - first):
        stacked = source[:, pl.ds(off_row + n * GROUP, GROUP), :].reshape(PARTS * GROUP, B)
        slot = n % 2
        product[slot] = jnp.dot(stacked, sol[first + n - shift], preferred_element_type=F32)
        for j in range(NB):
            target = codes[(first + n) * NB + j] - FIRST
            for i in range(ROWS):
                into = pl.ds(i * PARTS, PARTS)
                acc[target, into, :] += product[
                    slot, pl.ds(j * ROWS + i, PARTS, stride=GROUP), :
                ]


def leaf_level(codes, rhs, lead, sol, acc, stage, natural, weights, product):
    acc[...] = jnp.zeros_like(acc)
    collect(lead, stage, natural, weights, 0, 0, FIRST // 4)
    solve_level(
        codes, rhs, lead, weights, product, acc, natural, sol,
        0, FIRST, 0, 0, FIRST * ROWS, True,
    )


def later_levels(
    codes, where, rhs, top_rhs, acc_in, leaf_sol, rest,
    sol_hbm, part, acc, sol, stage, natural, weights, product, base, sems,
):
    stores = (
        pltpu.make_async_copy(leaf_sol, sol_hbm.at[pl.ds(0, FIRST)], sems.at[0]),
        pltpu.make_async_copy(sol, sol_hbm.at[pl.ds(FIRST, LATER)], sems.at[1]),
    )
    stores[0].start()
    acc[...] = acc_in[...]
    collect(rest, stage, natural, weights, 0, 0, LATER_PAD // 4)
    collect(rest, stage, natural, weights, TOP_ROW, LATER_PAD, TOP_BLOCKS // 4)
    for first, end in LEVELS[1:]:
        off_row = LATER_PAD * ROWS + (first - FIRST) * GROUP
        solve_level(
            codes, rhs, rest, weights, product, acc, natural, sol,
            first, end, FIRST, first - FIRST, off_row, False,
        )
    stores[1].start()

    for t in range(TOP):
        own = jnp.where(where[0] == t, top_rhs[...].astype(F32), 0.0)
        base[t] = own - summed(acc, natural, SUB - FIRST + t)
    for k in range(TOP):
        at = LATER_PAD + k
        solved = jnp.dot(weights[at + START[k]], base[k].astype(BF16), preferred_element_type=F32)
        solved = solved.astype(BF16)
        part[k] = solved
        for t in range(k + 1, TOP):
            base[t] -= jnp.dot(weights[at + START[t]], solved, preferred_element_type=F32)
    for store in stores:
        store.wait()


def pack_rows(row, diag, off, factor, inverse, lead, rest, own, factor_rows, inverse_rows, spread, sems):
    lead_diag, lead_off = FIRST * ROWS, FIRST * GROUP
    rest_diag, rest_off = LATER * ROWS, LATER * GROUP
    rest_at = LATER_PAD * ROWS
    copies = (
        pltpu.make_async_copy(factor, factor_rows, sems.at[0]),
        pltpu.make_async_copy(inverse, inverse_rows, sems.at[1]),
        pltpu.make_async_copy(diag.at[pl.ds(0, lead_diag)], lead.at[pl.ds(0, lead_diag)], sems.at[2]),
        pltpu.make_async_copy(off.at[pl.ds(0, lead_off)], lead.at[pl.ds(lead_diag, lead_off)], sems.at[3]),
        pltpu.make_async_copy(diag.at[pl.ds(lead_diag, rest_diag)], rest.at[pl.ds(0, rest_diag)], sems.at[4]),
        pltpu.make_async_copy(off.at[pl.ds(lead_off, rest_off)], rest.at[pl.ds(rest_at, rest_off)], sems.at[5]),
    )
    for copy in copies:
        copy.start()
    gap = (LATER_PAD - LATER) * ROWS
    rest[pl.ds(rest_at - gap, gap), :] = jnp.zeros((gap, B), BF16)
    copies[0].wait()
    copies[1].wait()
    for i in range(ROWS):
        line = inverse_rows[...].astype(F32)[i : i + 1]
        spread[pl.ds(i, TOP, stride=ROWS), :] = jnp.broadcast_to(line, (TOP, B))
    block = lax.broadcasted_iota(jnp.int32, (TOP * ROWS, B), 0) // ROWS
    top = jnp.where(block == row[0], spread[...], factor_rows[...].astype(F32))
    own[...] = top.astype(BF16)
    for copy in copies[2:]:
        copy.wait()


VMEM = pl.BlockSpec(memory_space=pltpu.VMEM)
SMEM = pl.BlockSpec(memory_space=pltpu.SMEM)
HBM = pl.BlockSpec(memory_space=pl.ANY)
WORK = (
    pltpu.VMEM((PARTS * GROUP, B), F32),
    pltpu.VMEM((4, B, B), F32),
)
ACC_SHAPE = (SUB - FIRST + TOP, B, B)


def cost(blocks, nbytes):
    return pl.CostEstimate(flops=2 * B**3 * blocks, bytes_accessed=nbytes, transcendentals=0)


def run_pack(row, diag, off, factor, inverse):
    return pl.pallas_call(
        pack_rows,
        out_shape=[
            jax.ShapeDtypeStruct((rows, B), BF16) for rows in (LEAD_ROWS, TOP_ROW, TOP * ROWS)
        ],
        in_specs=[SMEM] + [HBM] * 4,
        out_specs=[VMEM] * 3,
        scratch_shapes=[
            pltpu.VMEM((TOP * ROWS, B), BF16),
            pltpu.VMEM((ROWS, B), BF16),
            pltpu.VMEM((TOP * ROWS, B), F32),
            pltpu.SemaphoreType.DMA((6,)),
        ],
        compiler_params=pltpu.CompilerParams(vmem_limit_bytes=56 << 20),
        cost_estimate=cost(0, 1 << 19),
    )(row, diag, off, factor, inverse)


def run_leaves(codes, rhs, lead):
    return pl.pallas_call(
        leaf_level,
        out_shape=(
            jax.ShapeDtypeStruct((FIRST, B, B), BF16),
            jax.ShapeDtypeStruct(ACC_SHAPE, F32),
        ),
        in_specs=[SMEM, VMEM, VMEM],
        out_specs=(VMEM, VMEM),
        scratch_shapes=[
            *WORK,
            pltpu.VMEM((FIRST, B, B), BF16),
            pltpu.VMEM((2, PARTS * GROUP, B), F32),
        ],
        compiler_params=pltpu.CompilerParams(vmem_limit_bytes=16 << 20),
        cost_estimate=cost(FIRST * (1 + NB), 8 << 20),
    )(codes, rhs, lead)


def run_later(codes, where, rhs, top_rhs, acc, leaf_sol, rest):
    return pl.pallas_call(
        later_levels,
        out_shape=(
            jax.ShapeDtypeStruct((SUB, B, B), BF16),
            jax.ShapeDtypeStruct((TOP, B, B), BF16),
        ),
        in_specs=[SMEM, SMEM] + [VMEM] * 5,
        out_specs=(HBM, VMEM),
        scratch_shapes=[
            pltpu.VMEM(ACC_SHAPE, F32),
            pltpu.VMEM((LATER, B, B), BF16),
            *WORK,
            pltpu.VMEM((LATER_PAD + TOP_BLOCKS, B, B), BF16),
            pltpu.VMEM((2, PARTS * GROUP, B), F32),
            pltpu.VMEM((TOP, B, B), F32),
            pltpu.SemaphoreType.DMA((2,)),
        ],
        compiler_params=pltpu.CompilerParams(vmem_limit_bytes=16 << 20),
        cost_estimate=cost(LATER * (1 + NB) + TOP * (TOP + 1) // 2, 8 << 20),
    )(codes, where, rhs, top_rhs, acc, leaf_sol, rest)


def shift(x, axis, k):
    size = lax.axis_size(axis)
    return lax.ppermute(x, axis, [(n, (n + k) % size) for n in range(size)])


def put(buffer, x, *start):
    start = start + (0,) * (buffer.ndim - len(start))
    shape = (1,) * (buffer.ndim - x.ndim) + x.shape
    return lax.dynamic_update_slice(buffer, x.reshape(shape), start)


def gather_z_then_y(x, other, after):
    y, z = lax.axis_index("y"), lax.axis_index("z")
    own = put(jnp.zeros((NZ, *x.shape), x.dtype), x, z)
    right, left = x, x
    for k in range(1, 4):
        right, left = shift(right, "z", 1), shift(left, "z", -1)
        if k == after:
            right, left, other = lax.optimization_barrier((right, left, other))
        own = put(put(own, right, (z - k) % NZ), left, (z + k) % NZ)
    own = put(own, shift(right, "z", 1), (z + 4) % NZ)
    half = NZ // 2
    every = put(jnp.zeros((NY, *own.shape), x.dtype), own, y)
    right, left = shift(own, "y", 1), shift(own, "y", -1)
    every = put(put(every, right, (y - 1) % NY), left, (y + 1) % NY)
    every = put(every, shift(right[:half], "y", 1)[None], (y + 2) % NY)
    every = put(every, shift(left[half:], "y", -1)[None], (y + 2) % NY, half)
    return every.reshape(PARTS, *x.shape), other


def gather_y(x):
    y = lax.axis_index("y")
    own = put(jnp.zeros((NY, *x.shape), x.dtype), x, y)
    for k in (1, -1, 2):
        own = put(own, shift(x, "y", k), (y - k) % NY)
    return own


def gather_z(own):
    x, z = own[0], lax.axis_index("z")
    half = NY // 2
    every = put(jnp.zeros((NY, NZ, *x.shape), x.dtype), own[:, None], 0, z)
    right, left = own, own
    for k in range(1, 4):
        right, left = shift(right, "z", 1), shift(left, "z", -1)
        every = put(put(every, right[:, None], 0, (z - k) % NZ), left[:, None], 0, (z + k) % NZ)
    every = put(every, shift(right[:half], "z", 1)[:, None], 0, (z + 4) % NZ)
    every = put(every, shift(left[half:], "z", -1)[:, None], half, (z + 4) % NZ)
    return every.reshape(PARTS, *x.shape)


def gather_row(x):
    chip = lax.axis_index("x")
    pair = lax.all_gather(x, "core", axis=0)
    every = put(jnp.zeros((lax.axis_size("x"), *pair.shape), x.dtype), pair, chip)
    for k in (1, -1, 2):
        every = put(every, shift(pair, "x", k), (chip - k) % lax.axis_size("x"))
    return every.reshape(TOP, *x.shape)


def local(local_rhs, top_rhs, diag_inv, top_inv, off_blocks, top_factor, targets):
    position = lax.axis_index(ROW)
    lead, rest, top_rows = run_pack(
        position[None],
        diag_inv.reshape(-1, B),
        off_blocks.reshape(-1, B),
        top_factor.reshape(-1, B),
        top_inv.reshape(-1, B),
    )
    top_all = gather_row(top_rows)
    rest = jnp.concatenate([rest, *(top_all[t, : WIDTH[t] * ROWS] for t in range(TOP))], axis=0)
    lead_all, rest = gather_z_then_y(lead, rest, 1)
    rest_all = gather_z(gather_y(rest))
    codes = targets.reshape(-1)
    leaf_sol, acc = run_leaves(codes, local_rhs, lead_all)
    sol, addends = run_later(codes, position[None], local_rhs, top_rhs[0], acc, leaf_sol, rest_all)
    parts = lax.all_to_all(addends, ROW, 0, 0, tiled=True)
    own_top = jnp.sum(parts.astype(F32), axis=0, keepdims=True).astype(BF16)
    return sol, own_top


def solution(mesh):
    mesh = jax.sharding.Mesh(mesh.devices.reshape(4, 2, NY, NZ), (*ROW, *RHS))
    in_specs = (
        P(ROW, None, RHS),
        P(ROW, None, RHS),
        P(ROW, RHS, None),
        P(ROW, RHS, None),
        P(ROW, None, RHS, None),
        P(ROW, None, RHS, None),
        P(ROW, None),
    )
    out_specs = (P(ROW, None, RHS), P(ROW, None, RHS))
    return jax.shard_map(local, mesh=mesh, in_specs=in_specs, out_specs=out_specs, check_vma=False)
```

```python
import jax
import jax.numpy as jnp
from jax import lax
from jax.experimental import pallas as pl
from jax.experimental.pallas import tpu as pltpu
from jax.sharding import PartitionSpec as P

SUB = 42
LEVELS = ((0, 24), (24, 36), (36, 42))
B = 128
NB = 4
TOP = 8
PARTS = 32
ROWS = B // PARTS
GROUP = 16
FIRST = LEVELS[0][1]
LATER = SUB - FIRST
LATER_PAD = -(-LATER // 4) * 4
WIDTH = tuple(t - t % 2 + 2 for t in range(TOP))
START = tuple(sum(WIDTH[:t]) for t in range(TOP))
TOP_BLOCKS = sum(WIDTH)
LEAD_ROWS = FIRST * (1 + NB) * ROWS
REST_ROWS = (LATER_PAD + LATER * NB + TOP_BLOCKS) * ROWS
TOP_ROW = (LATER_PAD + LATER * NB) * ROWS
NY, NZ = 4, 8
ROW, RHS = ("x", "core"), ("y", "z")
F32 = jnp.float32
BF16 = jnp.bfloat16


def collect(source, stage, natural, weights, first_row, first_block, groups):
    for g in range(groups):
        slot = g % 2
        rows = source[:, pl.ds(first_row + g * GROUP, GROUP), :].astype(F32)
        stage[slot] = rows.reshape(PARTS * GROUP, B)
        for q in range(GROUP // ROWS):
            for i in range(ROWS):
                natural[slot * 4 + q, pl.ds(i, PARTS, stride=ROWS), :] = stage[
                    slot, pl.ds(q * ROWS + i, PARTS, stride=GROUP), :
                ]
            weights[first_block + g * 4 + q] = natural[slot * 4 + q].astype(BF16)


def summed(acc, natural, target):
    slot = target % 8
    for i in range(ROWS):
        natural[slot, pl.ds(i, PARTS, stride=ROWS), :] = acc[target, pl.ds(i * PARTS, PARTS), :]
    return natural[slot]


def solve_level(
    codes, rhs, source, weights, product, acc, natural, sol,
    first, end, shift, first_block, off_row, is_leaf,
):
    for n in range(end - first):
        values = rhs[first + n]
        if not is_leaf:
            values = (values.astype(F32) - summed(acc, natural, first + n - FIRST)).astype(BF16)
        solved = jnp.dot(weights[first_block + n], values, preferred_element_type=F32)
        sol[first + n - shift] = solved.astype(BF16)
    for n in range(end - first):
        stacked = source[:, pl.ds(off_row + n * GROUP, GROUP), :].reshape(PARTS * GROUP, B)
        slot = n % 2
        product[slot] = jnp.dot(stacked, sol[first + n - shift], preferred_element_type=F32)
        for j in range(NB):
            target = codes[(first + n) * NB + j] - FIRST
            for i in range(ROWS):
                into = pl.ds(i * PARTS, PARTS)
                acc[target, into, :] += product[
                    slot, pl.ds(j * ROWS + i, PARTS, stride=GROUP), :
                ]


def leaf_level(codes, rhs, lead, sol, acc, stage, natural, weights, product):
    acc[...] = jnp.zeros_like(acc)
    collect(lead, stage, natural, weights, 0, 0, FIRST // 4)
    solve_level(
        codes, rhs, lead, weights, product, acc, natural, sol,
        0, FIRST, 0, 0, FIRST * ROWS, True,
    )


def later_levels(
    codes, where, rhs, top_rhs, acc_in, leaf_sol, rest,
    sol_hbm, part, acc, sol, stage, natural, weights, product, base, sems,
):
    stores = (
        pltpu.make_async_copy(leaf_sol, sol_hbm.at[pl.ds(0, FIRST)], sems.at[0]),
        pltpu.make_async_copy(sol, sol_hbm.at[pl.ds(FIRST, LATER)], sems.at[1]),
    )
    stores[0].start()
    acc[...] = acc_in[...]
    collect(rest, stage, natural, weights, 0, 0, LATER_PAD // 4)
    collect(rest, stage, natural, weights, TOP_ROW, LATER_PAD, TOP_BLOCKS // 4)
    for first, end in LEVELS[1:]:
        off_row = LATER_PAD * ROWS + (first - FIRST) * GROUP
        solve_level(
            codes, rhs, rest, weights, product, acc, natural, sol,
            first, end, FIRST, first - FIRST, off_row, False,
        )
    stores[1].start()

    for t in range(TOP):
        own = jnp.where(where[0] == t, top_rhs[...].astype(F32), 0.0)
        base[t] = own - summed(acc, natural, SUB - FIRST + t)
    for k in range(TOP):
        at = LATER_PAD + k
        solved = jnp.dot(weights[at + START[k]], base[k].astype(BF16), preferred_element_type=F32)
        solved = solved.astype(BF16)
        part[k] = solved
        for t in range(k + 1, TOP):
            base[t] -= jnp.dot(weights[at + START[t]], solved, preferred_element_type=F32)
    for store in stores:
        store.wait()


def pack_rows(row, diag, off, factor, inverse, lead, rest, own, factor_rows, inverse_rows, spread, sems):
    lead_diag, lead_off = FIRST * ROWS, FIRST * GROUP
    rest_diag, rest_off = LATER * ROWS, LATER * GROUP
    rest_at = LATER_PAD * ROWS
    copies = (
        pltpu.make_async_copy(factor, factor_rows, sems.at[0]),
        pltpu.make_async_copy(inverse, inverse_rows, sems.at[1]),
        pltpu.make_async_copy(diag.at[pl.ds(0, lead_diag)], lead.at[pl.ds(0, lead_diag)], sems.at[2]),
        pltpu.make_async_copy(off.at[pl.ds(0, lead_off)], lead.at[pl.ds(lead_diag, lead_off)], sems.at[3]),
        pltpu.make_async_copy(diag.at[pl.ds(lead_diag, rest_diag)], rest.at[pl.ds(0, rest_diag)], sems.at[4]),
        pltpu.make_async_copy(off.at[pl.ds(lead_off, rest_off)], rest.at[pl.ds(rest_at, rest_off)], sems.at[5]),
    )
    for copy in copies:
        copy.start()
    gap = (LATER_PAD - LATER) * ROWS
    rest[pl.ds(rest_at - gap, gap), :] = jnp.zeros((gap, B), BF16)
    copies[0].wait()
    copies[1].wait()
    for i in range(ROWS):
        line = inverse_rows[...].astype(F32)[i : i + 1]
        spread[pl.ds(i, TOP, stride=ROWS), :] = jnp.broadcast_to(line, (TOP, B))
    block = lax.broadcasted_iota(jnp.int32, (TOP * ROWS, B), 0) // ROWS
    top = jnp.where(block == row[0], spread[...], factor_rows[...].astype(F32))
    own[...] = top.astype(BF16)
    for copy in copies[2:]:
        copy.wait()


VMEM = pl.BlockSpec(memory_space=pltpu.VMEM)
SMEM = pl.BlockSpec(memory_space=pltpu.SMEM)
HBM = pl.BlockSpec(memory_space=pl.ANY)
WORK = (
    pltpu.VMEM((2, PARTS * GROUP, B), F32),
    pltpu.VMEM((8, B, B), F32),
)
ACC_SHAPE = (SUB - FIRST + TOP, B, B)


def cost(blocks, nbytes):
    return pl.CostEstimate(flops=2 * B**3 * blocks, bytes_accessed=nbytes, transcendentals=0)


def run_pack(row, diag, off, factor, inverse):
    return pl.pallas_call(
        pack_rows,
        out_shape=[
            jax.ShapeDtypeStruct((rows, B), BF16) for rows in (LEAD_ROWS, TOP_ROW, TOP * ROWS)
        ],
        in_specs=[SMEM] + [HBM] * 4,
        out_specs=[VMEM] * 3,
        scratch_shapes=[
            pltpu.VMEM((TOP * ROWS, B), BF16),
            pltpu.VMEM((ROWS, B), BF16),
            pltpu.VMEM((TOP * ROWS, B), F32),
            pltpu.SemaphoreType.DMA((6,)),
        ],
        compiler_params=pltpu.CompilerParams(vmem_limit_bytes=56 << 20),
        cost_estimate=cost(0, 1 << 19),
    )(row, diag, off, factor, inverse)


def run_leaves(codes, rhs, lead):
    return pl.pallas_call(
        leaf_level,
        out_shape=(
            jax.ShapeDtypeStruct((FIRST, B, B), BF16),
            jax.ShapeDtypeStruct(ACC_SHAPE, F32),
        ),
        in_specs=[SMEM, VMEM, VMEM],
        out_specs=(VMEM, VMEM),
        scratch_shapes=[
            *WORK,
            pltpu.VMEM((FIRST, B, B), BF16),
            pltpu.VMEM((2, PARTS * GROUP, B), F32),
        ],
        compiler_params=pltpu.CompilerParams(vmem_limit_bytes=16 << 20),
        cost_estimate=cost(FIRST * (1 + NB), 8 << 20),
    )(codes, rhs, lead)


def run_later(codes, where, rhs, top_rhs, acc, leaf_sol, rest):
    return pl.pallas_call(
        later_levels,
        out_shape=(
            jax.ShapeDtypeStruct((SUB, B, B), BF16),
            jax.ShapeDtypeStruct((TOP, B, B), BF16),
        ),
        in_specs=[SMEM, SMEM] + [VMEM] * 5,
        out_specs=(HBM, VMEM),
        scratch_shapes=[
            pltpu.VMEM(ACC_SHAPE, F32),
            pltpu.VMEM((LATER, B, B), BF16),
            *WORK,
            pltpu.VMEM((LATER_PAD + TOP_BLOCKS, B, B), BF16),
            pltpu.VMEM((2, PARTS * GROUP, B), F32),
            pltpu.VMEM((TOP, B, B), F32),
            pltpu.SemaphoreType.DMA((2,)),
        ],
        compiler_params=pltpu.CompilerParams(vmem_limit_bytes=16 << 20),
        cost_estimate=cost(LATER * (1 + NB) + TOP * (TOP + 1) // 2, 8 << 20),
    )(codes, where, rhs, top_rhs, acc, leaf_sol, rest)


def shift(x, axis, k):
    size = lax.axis_size(axis)
    return lax.ppermute(x, axis, [(n, (n + k) % size) for n in range(size)])


def put(buffer, x, *start):
    start = start + (0,) * (buffer.ndim - len(start))
    shape = (1,) * (buffer.ndim - x.ndim) + x.shape
    return lax.dynamic_update_slice(buffer, x.reshape(shape), start)


def gather_z_then_y(x, other, after):
    y, z = lax.axis_index("y"), lax.axis_index("z")
    own = put(jnp.zeros((NZ, *x.shape), x.dtype), x, z)
    right, left = x, x
    for k in range(1, 4):
        right, left = shift(right, "z", 1), shift(left, "z", -1)
        if k == after:
            right, left, other = lax.optimization_barrier((right, left, other))
        own = put(put(own, right, (z - k) % NZ), left, (z + k) % NZ)
    own = put(own, shift(right, "z", 1), (z + 4) % NZ)
    half = NZ // 2
    every = put(jnp.zeros((NY, *own.shape), x.dtype), own, y)
    right, left = shift(own, "y", 1), shift(own, "y", -1)
    every = put(put(every, right, (y - 1) % NY), left, (y + 1) % NY)
    every = put(every, shift(right[:half], "y", 1)[None], (y + 2) % NY)
    every = put(every, shift(left[half:], "y", -1)[None], (y + 2) % NY, half)
    return every.reshape(PARTS, *x.shape), other


def gather_y(x):
    y = lax.axis_index("y")
    own = put(jnp.zeros((NY, *x.shape), x.dtype), x, y)
    for k in (1, -1, 2):
        own = put(own, shift(x, "y", k), (y - k) % NY)
    return own


def gather_z(own):
    x, z = own[0], lax.axis_index("z")
    half = NY // 2
    every = put(jnp.zeros((NY, NZ, *x.shape), x.dtype), own[:, None], 0, z)
    right, left = own, own
    for k in range(1, 4):
        right, left = shift(right, "z", 1), shift(left, "z", -1)
        every = put(put(every, right[:, None], 0, (z - k) % NZ), left[:, None], 0, (z + k) % NZ)
    every = put(every, shift(right[:half], "z", 1)[:, None], 0, (z + 4) % NZ)
    every = put(every, shift(left[half:], "z", -1)[:, None], half, (z + 4) % NZ)
    return every.reshape(PARTS, *x.shape)


def gather_row(x):
    chip = lax.axis_index("x")
    pair = lax.all_gather(x, "core", axis=0)
    every = put(jnp.zeros((lax.axis_size("x"), *pair.shape), x.dtype), pair, chip)
    for k in (1, -1, 2):
        every = put(every, shift(pair, "x", k), (chip - k) % lax.axis_size("x"))
    return every.reshape(TOP, *x.shape)


def local(local_rhs, top_rhs, diag_inv, top_inv, off_blocks, top_factor, targets):
    position = lax.axis_index(ROW)
    lead, rest, top_rows = run_pack(
        position[None],
        diag_inv.reshape(-1, B),
        off_blocks.reshape(-1, B),
        top_factor.reshape(-1, B),
        top_inv.reshape(-1, B),
    )
    top_all = gather_row(top_rows)
    rest = jnp.concatenate([rest, *(top_all[t, : WIDTH[t] * ROWS] for t in range(TOP))], axis=0)
    lead_all, rest = gather_z_then_y(lead, rest, 1)
    rest_all = gather_z(gather_y(rest))
    codes = targets.reshape(-1)
    leaf_sol, acc = run_leaves(codes, local_rhs, lead_all)
    sol, addends = run_later(codes, position[None], local_rhs, top_rhs[0], acc, leaf_sol, rest_all)
    parts = lax.all_to_all(addends, ROW, 0, 0, tiled=True)
    own_top = jnp.sum(parts.astype(F32), axis=0, keepdims=True).astype(BF16)
    return sol, own_top


def solution(mesh):
    mesh = jax.sharding.Mesh(mesh.devices.reshape(4, 2, NY, NZ), (*ROW, *RHS))
    in_specs = (
        P(ROW, None, RHS),
        P(ROW, None, RHS),
        P(ROW, RHS, None),
        P(ROW, RHS, None),
        P(ROW, None, RHS, None),
        P(ROW, None, RHS, None),
        P(ROW, None),
    )
    out_specs = (P(ROW, None, RHS), P(ROW, None, RHS))
    return jax.shard_map(local, mesh=mesh, in_specs=in_specs, out_specs=out_specs, check_vma=False)
```
